32 devices in a mesh: tile: 8 (over y, x, core), bin: 4 (over z).
Axes of the slice: x: 2, y: 2, z: 4, core: 2. Of those that a mesh axis runs over, the one named last changes fastest.
Arguments:
- dust_density: float32 [64, 64, 512], P('bin', 'tile'), may hold values from 0.05 to 2
- dust_vr: float32 [64, 64, 512], P('bin', 'tile'), may hold values from -1 to 1
- dust_va: float32 [64, 64, 512], P('bin', 'tile'), may hold values from -1 to 1
- gas_density: float32 [64, 512], P('tile'), may hold values from 0.5 to 2
- gas_vr: float32 [64, 512], P('tile'), may hold values from -1 to 1
- gas_va: float32 [64, 512], P('tile'), may hold values from -1 to 1
- stop_time: float32 [64], P('bin'), may hold values from 0.05 to 20
- gain_coef: bfloat16 [64, 64, 64], P('bin'), may hold values from -0.09375 to 0.09375
Outputs:
- density_out: float32 [64, 64, 512], P('bin', 'tile')
- vr_out: float32 [64, 64, 512], P('bin', 'tile')
- va_out: float32 [64, 64, 512], P('bin', 'tile')
- gas_vr_out: float32 [64, 512], P('tile')
- gas_va_out: float32 [64, 512], P('tile')
The draws below stay inside these ranges and needn't reach their ends.
All inputs are finite; a program needn't handle non-finite values.
Results may differ from the reference program's by a relative error of at most 0.0017.
Values may be sent and summed in bfloat16 or wider, within the bound.
No kernel may reach another device: no remote copies, remote signals or barrier semaphores. Data moves between devices by JAX's collectives and lax.ppermute only.
A program may use at most 64 MiB of HBM per device.

```python
import math
import jax
import jax.numpy as jnp
from jax import lax

NA = 512
BINS = 64
NR = 64


def steps_of(own_key, shape, cuts, low, high):
    def one(position, blocks):
        steps = jax.random.uniform(jax.random.fold_in(jax.random.fold_in(own_key, 6), position), (blocks,), jnp.float32, low / len(cuts), high / len(cuts))
        return jnp.repeat(jnp.exp(steps), shape[position] // blocks).reshape((-1,) + (1,) * (len(shape) - position - 1))

    factor_of = one(*cuts[0])
    for cut in cuts[1:]:
        factor_of = factor_of * one(*cut)
    return factor_of


def normal_values(key, extent, spread, reach, pieces=(), dtype=jnp.bfloat16):
    values = jax.random.normal(key, extent, jnp.float32) * spread
    if len(pieces) > 0:
        values = steps_of(key, extent, pieces, -0.22, 0.18) * values
    return jnp.clip(values, min=-reach, max=reach).astype(dtype)


def setup_inputs(seed: int = 0) -> dict:
    keys = jax.random.split(jax.random.key(seed), 9)
    return {
        "dust_density": jnp.clip(jnp.exp(math.log(2.0) - 3.6888794 * jax.random.uniform(keys[0], (BINS, NR, NA), jnp.float32) ** steps_of(keys[0], (BINS, NR, NA), ((0, 4), (1, 8)), -0.2, 0.2)), 0.05, 2.0),
        "dust_vr": jnp.clip(jax.random.uniform(keys[1], (BINS, NR, NA), jnp.float32, -1.0, 1.0) * steps_of(keys[1], (BINS, NR, NA), ((0, 4), (1, 8)), -0.4, 0.0), -1.0, 1.0),
        "dust_va": jnp.clip(jax.random.uniform(keys[2], (BINS, NR, NA), jnp.float32, -1.0, 1.0) * steps_of(keys[2], (BINS, NR, NA), ((0, 4), (1, 8)), -0.4, 0.0), -1.0, 1.0),
        "gas_density": jnp.clip(0.5 + 1.5 * jax.random.uniform(keys[3], (NR, NA), jnp.float32) ** steps_of(keys[3], (NR, NA), ((0, 8),), -0.2, 0.2), 0.5, 2.0),
        "gas_vr": jnp.clip(jax.random.uniform(keys[4], (NR, NA), jnp.float32, -1.0, 1.0) * steps_of(keys[4], (NR, NA), ((0, 8),), -0.4, 0.0), -1.0, 1.0),
        "gas_va": jnp.clip(jax.random.uniform(keys[5], (NR, NA), jnp.float32, -1.0, 1.0) * steps_of(keys[5], (NR, NA), ((0, 8),), -0.4, 0.0), -1.0, 1.0),
        "stop_time": jnp.clip(jnp.exp(math.log(20.0) - 5.9914645 * jax.random.uniform(keys[6], (BINS,), jnp.float32) ** steps_of(keys[6], (BINS,), ((0, 4),), -0.2, 0.2)), 0.05, 20.0),
        "gain_coef": normal_values(keys[7], (BINS, BINS, BINS), (BINS * BINS) ** -0.5, 0.09375, ((0, 4),)),
    }


COURANT = 0.2
COAGULATION = 0.5


def minmod(first, second):
    smaller = jnp.sign(first) * jnp.minimum(jnp.abs(first), jnp.abs(second))
    return jnp.where(first * second > 0, smaller, jnp.zeros_like(first))


def faces_div(values, speeds, along):
    length = values.shape[along]

    def part(array, lower, upper_cut):
        return lax.slice_in_dim(array, lower, length - upper_cut, axis=along)

    slope = minmod(part(values, 1, 1) - part(values, 0, 2), part(values, 2, 0) - part(values, 1, 1))
    centre = part(values, 1, 1)
    centre_speed = part(speeds, 1, 1)
    inner_len = length - 2

    def sub(array, lower, upper_cut):
        return lax.slice_in_dim(array, lower, inner_len - upper_cut, axis=along)

    speed = 0.5 * (sub(centre_speed, 0, 1) + sub(centre_speed, 1, 0))
    left = sub(centre, 0, 1) + 0.5 * (1.0 - speed * COURANT) * sub(slope, 0, 1)
    right = sub(centre, 1, 0) - 0.5 * (1.0 + speed * COURANT) * sub(slope, 1, 0)
    flux = jnp.maximum(speed, 0.0) * left + jnp.minimum(speed, 0.0) * right
    face_count = inner_len - 1
    return lax.slice_in_dim(flux, 1, face_count, axis=along) - lax.slice_in_dim(flux, 0, face_count - 1, axis=along)


def wrap_azimuth(field):
    return jnp.concatenate([field[..., -2:], field, field[..., :2]], axis=-1)


def reference(dust_density, dust_vr, dust_va, gas_density, gas_vr, gas_va, stop_time, gain_coef):
    padded_rho = jnp.pad(dust_density, ((0, 0), (2, 2), (0, 0)))
    padded_speed = jnp.pad(dust_vr, ((0, 0), (2, 2), (0, 0)))
    radial_div = faces_div(padded_rho, padded_speed, 1)
    azimuth_div = faces_div(wrap_azimuth(dust_density), wrap_azimuth(dust_va), 2)
    density_adv = dust_density - COURANT * (radial_div + azimuth_div)
    drag_rate = 1.0 / stop_time
    coupling = drag_rate / (1.0 + drag_rate)
    weight = density_adv * coupling[:, None, None]
    sum_radial = jnp.sum(weight * dust_vr, axis=0)
    sum_azimuth = jnp.sum(weight * dust_va, axis=0)
    sum_weight = jnp.sum(weight, axis=0)
    denom = gas_density + sum_weight
    gas_vr_out = (gas_density * gas_vr + sum_radial) / denom
    gas_va_out = (gas_density * gas_va + sum_azimuth) / denom
    rate_col = drag_rate[:, None, None]
    vr_out = (dust_vr + rate_col * gas_vr_out[None]) / (1.0 + rate_col)
    va_out = (dust_va + rate_col * gas_va_out[None]) / (1.0 + rate_col)
    bin_total = dust_density.shape[0]
    density_low = density_adv.astype(jnp.bfloat16).reshape(bin_total, -1)
    density_wide = density_low.astype(jnp.float32)

    def one_bin(coef_slice):
        inner = jnp.dot(coef_slice, density_low, preferred_element_type=jnp.float32)
        return jnp.sum(density_wide * inner, axis=0)

    gain = lax.map(one_bin, gain_coef).reshape(density_adv.shape)
    density_out = density_adv + COAGULATION * gain
    return density_out, vr_out, va_out, gas_vr_out, gas_va_out
```

```python
import jax
import jax.numpy as jnp
from jax import lax
from jax.experimental import pallas as pl
from jax.experimental.pallas import tpu as pltpu
from jax.sharding import PartitionSpec as P

COURANT = 0.2
COAGULATION = 0.5
HALO = 2
F32 = jnp.float32
BF16 = jnp.bfloat16

VMEM = pl.BlockSpec(memory_space=pltpu.VMEM)
SMEM = pl.BlockSpec(memory_space=pltpu.SMEM)


def minmod(a, b):
    return jnp.maximum(jnp.minimum(a, b), 0.0) + jnp.minimum(jnp.maximum(a, b), 0.0)


def face_flux(low, low_slope, high, high_slope, u):
    cu = COURANT * u
    left = low + (0.5 - 0.5 * cu) * low_slope
    right = high - (0.5 + 0.5 * cu) * high_slope
    return jnp.maximum(u, 0.0) * left + jnp.minimum(u, 0.0) * right


def shift(x, by, axis):
    return pltpu.roll(x, by % x.shape[axis], axis)


def edge_kernel(rho_ref, vr_ref, to_a_ref, to_b_ref):
    rows = rho_ref.shape[1]
    even = lax.axis_index("tile") % 2 == 0
    up = (rho_ref[:, 0, :], rho_ref[:, 1, :], vr_ref[:, 0, :])
    down = (rho_ref[:, rows - 1, :], rho_ref[:, rows - 2, :], vr_ref[:, rows - 1, :])
    for n in range(3):
        to_a_ref[n] = jnp.where(even, down[n], up[n]).astype(BF16)
        to_b_ref[n] = jnp.where(even, up[n], down[n]).astype(BF16)


def radial(q, v, top, bottom):
    rows = q.shape[0]
    row = lax.broadcasted_iota(jnp.int32, q.shape, 0)
    first, last = row == 0, row == rows - 1
    q_next = jnp.where(last, bottom[0], shift(q, -1, 0))
    q_prev = jnp.where(first, top[0], shift(q, 1, 0))
    v_next = jnp.where(last, bottom[2], shift(v, -1, 0))
    v_prev = jnp.where(first, top[2], shift(v, 1, 0))
    d_next = q_next - q
    d_prev = q - q_prev
    s = minmod(d_prev, d_next)
    s_top = minmod(top[0] - top[1], d_prev)
    s_bottom = minmod(d_next, bottom[1] - bottom[0])
    s_prev = jnp.where(first, s_top, shift(s, 1, 0))
    s_next = jnp.where(last, s_bottom, shift(s, -1, 0))
    out = face_flux(q, s, q_next, s_next, 0.5 * (v + v_next))
    into = face_flux(q_prev, s_prev, q, s, 0.5 * (v_prev + v))
    return out - into


def azimuthal(q, v):
    q_next = shift(q, -1, 1)
    d = q_next - q
    s = minmod(shift(d, 1, 1), d)
    flux = face_flux(q, s, q_next, shift(s, -1, 1), 0.5 * (v + shift(v, -1, 1)))
    return flux - shift(flux, 1, 1)


def inner_kernel(rho_ref, vr_ref, va_ref, base_ref, low_ref, adv_ref):
    bins, rows, _ = rho_ref.shape

    def one_bin(b, carry):
        q = rho_ref[b]
        zero = jnp.zeros_like(q)
        base = q - COURANT * azimuthal(q, va_ref[b])
        base_ref[b] = base
        none = (zero, zero, zero)
        adv_ref[b] = base - COURANT * radial(q, vr_ref[b], none, none)
        return carry

    lax.fori_loop(0, bins, one_bin, 0)
    for n in range(rows - 2 * HALO):
        low_ref[n] = adv_ref[:, HALO + n, :].astype(BF16)


def outer_kernel(scal_ref, rho_ref, vr_ref, va_ref, base_ref, from_a_ref, from_b_ref, adv_ref, low_ref, sums_ref, top_ref, bottom_ref):
    bins, rows, _ = rho_ref.shape
    tile, tiles = lax.axis_index("tile"), lax.axis_size("tile")
    even = tile % 2 == 0
    has_top = jnp.where(tile > 0, 1.0, 0.0)
    has_bottom = jnp.where(tile < tiles - 1, 1.0, 0.0)
    for n in range(3):
        a, b = from_a_ref[n].astype(F32), from_b_ref[n].astype(F32)
        top_ref[n] = jnp.where(even, b, a) * has_top
        bottom_ref[n] = jnp.where(even, a, b) * has_bottom
    shape = sums_ref.shape[1:]

    def one_bin(b, sums):
        top = tuple(jnp.broadcast_to(top_ref[n, pl.ds(b, 1), :], shape) for n in range(3))
        bottom = tuple(jnp.broadcast_to(bottom_ref[n, pl.ds(b, 1), :], shape) for n in range(3))
        vr = vr_ref[b]
        adv = base_ref[b] - COURANT * radial(rho_ref[b], vr, top, bottom)
        adv_ref[b] = adv
        weight = adv * scal_ref[0, b]
        return (sums[0] + weight * vr, sums[1] + weight * va_ref[b], sums[2] + weight)

    zero = jnp.zeros(shape, F32)
    sums = lax.fori_loop(0, bins, one_bin, (zero, zero, zero))
    for n in range(3):
        sums_ref[n] = sums[n]
    for n, r in enumerate(edge_rows(rows)):
        low_ref[n] = adv_ref[:, r, :].astype(BF16)


def edge_rows(rows):
    return list(range(HALO)) + list(range(rows - HALO, rows))


def drag_kernel(scal_ref, sums_ref, more_ref, gas_ref, gvr_ref, gva_ref, vr_ref, va_ref, vr_out, va_out, gvr_out, gva_out):
    bins = vr_ref.shape[0]
    gas = gas_ref[...]
    denom = gas + (sums_ref[2] + more_ref[2])
    new_r = (gas * gvr_ref[...] + (sums_ref[0] + more_ref[0])) / denom
    new_a = (gas * gva_ref[...] + (sums_ref[1] + more_ref[1])) / denom
    gvr_out[...] = new_r
    gva_out[...] = new_a
    for b in range(bins):
        rate, scale = scal_ref[1, b], scal_ref[2, b]
        vr_out[b] = (vr_ref[b] + rate * new_r) * scale
        va_out[b] = (va_ref[b] + rate * new_a) * scale


def gather_low(parts, dens_ref, n_rows):
    here = lax.axis_index("bin")
    for offset, part in enumerate(parts):
        bins = part.shape[1]
        at = pl.multiple_of((here ^ offset) * bins, bins)
        for n in range(n_rows):
            dens_ref[n, pl.ds(at, bins), :] = part[n]


def gain_rows(coef_ref, dens_ref, gain_ref, bins, n_rows):
    total = dens_ref.shape[1]
    group = 8

    def one_row(n, carry):
        low = dens_ref[n]
        wide = low.astype(F32)
        acc = jnp.zeros((bins, low.shape[1]), F32)
        for i in range(0, total, group):
            inner = jnp.dot(coef_ref[i * bins:(i + group) * bins, :], low, preferred_element_type=F32)
            for g in range(group):
                acc = acc + inner[g * bins:(g + 1) * bins] * wide[i + g:i + g + 1]
        gain_ref[n] = acc
        return carry

    lax.fori_loop(0, n_rows, one_row, 0)


def inner_gain_kernel(coef_ref, *refs):
    *parts, gain_ref, dens_ref = refs
    n_rows, bins, _ = parts[0].shape
    gather_low(parts, dens_ref, n_rows)
    gain_rows(coef_ref, dens_ref, gain_ref, bins, n_rows)


def outer_gain_kernel(coef_ref, adv_ref, inner_ref, *refs):
    *parts, out_ref, dens_ref, gain_ref = refs
    n_rows, bins, _ = parts[0].shape
    rows = adv_ref.shape[1]
    gather_low(parts, dens_ref, n_rows)
    gain_rows(coef_ref, dens_ref, gain_ref, bins, n_rows)
    for n, r in enumerate(edge_rows(rows)):
        out_ref[:, r, :] = adv_ref[:, r, :] + COAGULATION * gain_ref[n]
    for n in range(rows - 2 * HALO):
        out_ref[:, HALO + n, :] = adv_ref[:, HALO + n, :] + COAGULATION * inner_ref[n]


def struct(shape, dtype=F32):
    return jax.ShapeDtypeStruct(shape, dtype)


def call(kernel, outs, specs, *args, scratch=()):
    return pl.pallas_call(
        kernel,
        out_shape=outs,
        in_specs=specs,
        out_specs=jax.tree.map(lambda _: VMEM, outs),
        scratch_shapes=scratch,
    )(*args)


def xor_pairs(axis, bit):
    return [(i, i ^ bit) for i in range(lax.axis_size(axis))]


def even_pairs(axis):
    return xor_pairs(axis, 1)


def odd_pairs(axis):
    count = lax.axis_size(axis)
    pairs = [(0, count - 1), (count - 1, 0)]
    for i in range(1, count - 1, 2):
        pairs += [(i, i + 1), (i + 1, i)]
    return pairs


def gather_bins(x):
    parts = {0: x}
    bit = lax.axis_size("bin") // 2
    while bit:
        parts.update({at ^ bit: lax.ppermute(part, "bin", xor_pairs("bin", bit)) for at, part in list(parts.items())})
        bit //= 2
    return [parts[at] for at in range(len(parts))]


def gather_direct(x):
    count = lax.axis_size("bin")
    sent = {at: lax.ppermute(x, "bin", xor_pairs("bin", at)) for at in range(count - 1, 0, -1)}
    return [x] + [sent[at] for at in range(1, count)]


def body(rho, vr, va, gas, gvr, gva, stop_time, coef):
    bins, rows, cells = rho.shape
    total = coef.shape[1]
    inner_rows, outer_rows = rows - 2 * HALO, 2 * HALO
    rate = 1.0 / stop_time
    scal = jnp.stack([rate / (1.0 + rate), rate, 1.0 / (1.0 + rate)])
    coef_rows = jnp.transpose(coef, (1, 0, 2)).reshape(total * bins, total)
    field = struct(rho.shape)

    halo = struct((3, bins, cells), BF16)
    to_a, to_b = call(edge_kernel, (halo, halo), [VMEM] * 2, rho, vr)
    from_b = lax.ppermute(to_b, "tile", odd_pairs("tile"))
    from_a = lax.ppermute(to_a, "tile", even_pairs("tile"))

    base, low_in = call(
        inner_kernel, (field, struct((inner_rows, bins, cells), BF16)), [VMEM] * 3, rho, vr, va,
        scratch=[pltpu.VMEM(rho.shape, F32)],
    )
    parts_in = gather_bins(low_in)

    adv, low_out, sums = call(
        outer_kernel, (field, struct((outer_rows, bins, cells), BF16), struct((3, rows, cells))),
        [SMEM] + [VMEM] * 6, scal, rho, vr, va, base, from_a, from_b,
        scratch=[pltpu.VMEM((3, bins, cells), F32)] * 2,
    )
    parts_out = gather_direct(low_out)

    bit = lax.axis_size("bin") // 2
    others = None
    step = 1
    while True:
        others = lax.ppermute(sums, "bin", xor_pairs("bin", step))
        step *= 2
        if step > bit:
            break
        sums = sums + others
    vr_out, va_out, gvr_out, gva_out = call(
        drag_kernel, (field, field, struct(gas.shape), struct(gas.shape)), [SMEM] + [VMEM] * 7,
        scal, sums, others, gas, gvr, gva, vr, va,
    )

    gain_in = call(
        inner_gain_kernel, struct((inner_rows, bins, cells)), [VMEM] * (1 + len(parts_in)), coef_rows, *parts_in,
        scratch=[pltpu.VMEM((inner_rows, total, cells), BF16)],
    )
    density_out = call(
        outer_gain_kernel, field, [VMEM] * (3 + len(parts_out)), coef_rows, adv, gain_in, *parts_out,
        scratch=[pltpu.VMEM((outer_rows, total, cells), BF16), pltpu.VMEM((outer_rows, bins, cells), F32)],
    )
    return density_out, vr_out, va_out, gvr_out, gva_out


def solution(mesh):
    field, flat = P("bin", "tile", None), P("tile", None)
    return jax.shard_map(
        body,
        mesh=mesh,
        in_specs=(field, field, field, flat, flat, flat, P("bin"), P("bin", None, None)),
        out_specs=(field, field, field, flat, flat),
        check_vma=False,
    )
```

```python
import jax
import jax.numpy as jnp
from jax import lax
from jax.experimental import pallas as pl
from jax.experimental.pallas import tpu as pltpu
from jax.sharding import PartitionSpec as P

COURANT = 0.2
COAGULATION = 0.5
HALO = 2
F32 = jnp.float32
BF16 = jnp.bfloat16

VMEM = pl.BlockSpec(memory_space=pltpu.VMEM)
SMEM = pl.BlockSpec(memory_space=pltpu.SMEM)


def minmod(a, b):
    return jnp.maximum(jnp.minimum(a, b), 0.0) + jnp.minimum(jnp.maximum(a, b), 0.0)


def face_flux(low, low_slope, high, high_slope, u):
    cu = COURANT * u
    left = low + (0.5 - 0.5 * cu) * low_slope
    right = high - (0.5 + 0.5 * cu) * high_slope
    return jnp.maximum(u, 0.0) * left + jnp.minimum(u, 0.0) * right


def shift(x, by, axis):
    return pltpu.roll(x, by % x.shape[axis], axis)


def edge_kernel(rho_ref, vr_ref, to_a_ref, to_b_ref):
    rows = rho_ref.shape[1]
    even = lax.axis_index("tile") % 2 == 0
    up = (rho_ref[:, 0, :], rho_ref[:, 1, :], vr_ref[:, 0, :])
    down = (rho_ref[:, rows - 1, :], rho_ref[:, rows - 2, :], vr_ref[:, rows - 1, :])
    for n in range(3):
        to_a_ref[n] = jnp.where(even, down[n], up[n]).astype(BF16)
        to_b_ref[n] = jnp.where(even, up[n], down[n]).astype(BF16)


def radial(q, v, top, bottom):
    rows = q.shape[0]
    row = lax.broadcasted_iota(jnp.int32, q.shape, 0)
    first, last = row == 0, row == rows - 1
    q_next = jnp.where(last, bottom[0], shift(q, -1, 0))
    q_prev = jnp.where(first, top[0], shift(q, 1, 0))
    v_next = jnp.where(last, bottom[2], shift(v, -1, 0))
    v_prev = jnp.where(first, top[2], shift(v, 1, 0))
    d_next = q_next - q
    d_prev = q - q_prev
    s = minmod(d_prev, d_next)
    s_top = minmod(top[0] - top[1], d_prev)
    s_bottom = minmod(d_next, bottom[1] - bottom[0])
    s_prev = jnp.where(first, s_top, shift(s, 1, 0))
    s_next = jnp.where(last, s_bottom, shift(s, -1, 0))
    out = face_flux(q, s, q_next, s_next, 0.5 * (v + v_next))
    into = face_flux(q_prev, s_prev, q, s, 0.5 * (v_prev + v))
    return out - into


def azimuthal(q, v):
    q_next = shift(q, -1, 1)
    d = q_next - q
    s = minmod(shift(d, 1, 1), d)
    flux = face_flux(q, s, q_next, shift(s, -1, 1), 0.5 * (v + shift(v, -1, 1)))
    return flux - shift(flux, 1, 1)


def inner_kernel(rho_ref, vr_ref, va_ref, base_ref, low_ref, adv_ref):
    bins, rows, _ = rho_ref.shape

    def one_bin(b, carry):
        q = rho_ref[b]
        zero = jnp.zeros_like(q)
        base = q - COURANT * azimuthal(q, va_ref[b])
        base_ref[b] = base
        none = (zero, zero, zero)
        adv_ref[b] = base - COURANT * radial(q, vr_ref[b], none, none)
        return carry

    lax.fori_loop(0, bins, one_bin, 0, unroll=True)
    for n in range(rows - 2 * HALO):
        low_ref[n] = adv_ref[:, HALO + n, :].astype(BF16)


def outer_kernel(scal_ref, rho_ref, vr_ref, va_ref, base_ref, from_a_ref, from_b_ref, adv_ref, low_ref, sums_ref, top_ref, bottom_ref):
    bins, rows, _ = rho_ref.shape
    tile, tiles = lax.axis_index("tile"), lax.axis_size("tile")
    even = tile % 2 == 0
    has_top = jnp.where(tile > 0, 1.0, 0.0)
    has_bottom = jnp.where(tile < tiles - 1, 1.0, 0.0)
    for n in range(3):
        a, b = from_a_ref[n].astype(F32), from_b_ref[n].astype(F32)
        top_ref[n] = jnp.where(even, b, a) * has_top
        bottom_ref[n] = jnp.where(even, a, b) * has_bottom
    shape = sums_ref.shape[1:]

    def one_bin(b, sums):
        top = tuple(jnp.broadcast_to(top_ref[n, pl.ds(b, 1), :], shape) for n in range(3))
        bottom = tuple(jnp.broadcast_to(bottom_ref[n, pl.ds(b, 1), :], shape) for n in range(3))
        vr = vr_ref[b]
        adv = base_ref[b] - COURANT * radial(rho_ref[b], vr, top, bottom)
        adv_ref[b] = adv
        weight = adv * scal_ref[0, b]
        return (sums[0] + weight * vr, sums[1] + weight * va_ref[b], sums[2] + weight)

    zero = jnp.zeros(shape, F32)
    sums = lax.fori_loop(0, bins, one_bin, (zero, zero, zero), unroll=True)
    for n in range(3):
        sums_ref[n] = sums[n]
    for n, r in enumerate(edge_rows(rows)):
        low_ref[n] = adv_ref[:, r, :].astype(BF16)


def edge_rows(rows):
    return list(range(HALO)) + list(range(rows - HALO, rows))


def drag_kernel(scal_ref, sums_ref, more_ref, gas_ref, gvr_ref, gva_ref, vr_ref, va_ref, vr_out, va_out, gvr_out, gva_out):
    bins = vr_ref.shape[0]
    gas = gas_ref[...]
    denom = gas + (sums_ref[2] + more_ref[2])
    new_r = (gas * gvr_ref[...] + (sums_ref[0] + more_ref[0])) / denom
    new_a = (gas * gva_ref[...] + (sums_ref[1] + more_ref[1])) / denom
    gvr_out[...] = new_r
    gva_out[...] = new_a
    for b in range(bins):
        rate, scale = scal_ref[1, b], scal_ref[2, b]
        vr_out[b] = (vr_ref[b] + rate * new_r) * scale
        va_out[b] = (va_ref[b] + rate * new_a) * scale


def gather_low(parts, dens_ref, n_rows):
    here = lax.axis_index("bin")
    for offset, part in enumerate(parts):
        bins = part.shape[1]
        at = pl.multiple_of((here ^ offset) * bins, bins)
        for n in range(n_rows):
            dens_ref[n, pl.ds(at, bins), :] = part[n]


def gain_rows(coef_ref, dens_ref, gain_ref, bins, n_rows):
    total = dens_ref.shape[1]
    group = 8

    def one_row(n, carry):
        low = dens_ref[n]
        wide = low.astype(F32)
        acc = jnp.zeros((bins, low.shape[1]), F32)
        for i in range(0, total, group):
            inner = jnp.dot(coef_ref[i * bins:(i + group) * bins, :], low, preferred_element_type=F32)
            for g in range(group):
                acc = acc + inner[g * bins:(g + 1) * bins] * wide[i + g:i + g + 1]
        gain_ref[n] = acc
        return carry

    lax.fori_loop(0, n_rows, one_row, 0)


def inner_gain_kernel(coef_ref, *refs):
    *parts, gain_ref, dens_ref = refs
    n_rows, bins, _ = parts[0].shape
    gather_low(parts, dens_ref, n_rows)
    gain_rows(coef_ref, dens_ref, gain_ref, bins, n_rows)


def outer_gain_kernel(coef_ref, adv_ref, inner_ref, *refs):
    *parts, out_ref, dens_ref, gain_ref = refs
    n_rows, bins, _ = parts[0].shape
    rows = adv_ref.shape[1]
    gather_low(parts, dens_ref, n_rows)
    gain_rows(coef_ref, dens_ref, gain_ref, bins, n_rows)
    for n, r in enumerate(edge_rows(rows)):
        out_ref[:, r, :] = adv_ref[:, r, :] + COAGULATION * gain_ref[n]
    for n in range(rows - 2 * HALO):
        out_ref[:, HALO + n, :] = adv_ref[:, HALO + n, :] + COAGULATION * inner_ref[n]


def struct(shape, dtype=F32):
    return jax.ShapeDtypeStruct(shape, dtype)


def call(kernel, outs, *args, scratch=(), scalars=0):
    specs = [SMEM] * scalars + [VMEM] * (len(args) - scalars)
    placed = [x if n < scalars else pltpu.with_memory_space_constraint(x, pltpu.VMEM) for n, x in enumerate(args)]
    return pl.pallas_call(
        kernel,
        out_shape=outs,
        in_specs=specs,
        out_specs=jax.tree.map(lambda _: VMEM, outs, is_leaf=lambda x: hasattr(x, "dtype")),
        scratch_shapes=scratch,
    )(*placed)


def xor_pairs(axis, bit):
    return [(i, i ^ bit) for i in range(lax.axis_size(axis))]


def even_pairs(axis):
    return xor_pairs(axis, 1)


def odd_pairs(axis):
    count = lax.axis_size(axis)
    pairs = [(0, count - 1), (count - 1, 0)]
    for i in range(1, count - 1, 2):
        pairs += [(i, i + 1), (i + 1, i)]
    return pairs


def gather_bins(x):
    parts = {0: x}
    bit = lax.axis_size("bin") // 2
    while bit:
        parts.update({at ^ bit: lax.ppermute(part, "bin", xor_pairs("bin", bit)) for at, part in list(parts.items())})
        bit //= 2
    return [parts[at] for at in range(len(parts))]


def gather_direct(x):
    count = lax.axis_size("bin")
    sent = {at: lax.ppermute(x, "bin", xor_pairs("bin", at)) for at in range(count - 1, 0, -1)}
    return [x] + [sent[at] for at in range(1, count)]


def body(rho, vr, va, gas, gvr, gva, stop_time, coef):
    bins, rows, cells = rho.shape
    total = coef.shape[1]
    inner_rows, outer_rows = rows - 2 * HALO, 2 * HALO
    rate = 1.0 / stop_time
    scal = jnp.stack([rate / (1.0 + rate), rate, 1.0 / (1.0 + rate)])
    coef_rows = jnp.transpose(coef, (1, 0, 2)).reshape(total * bins, total)
    field, kept = struct(rho.shape), pltpu.VMEM(rho.shape, F32)
    inner_low = pltpu.VMEM((inner_rows, bins, cells), BF16)
    outer_low = pltpu.VMEM((outer_rows, bins, cells), BF16)

    halo = pltpu.VMEM((3, bins, cells), BF16)
    to_a, to_b = call(edge_kernel, (halo, halo), rho, vr)
    from_b = lax.ppermute(to_b, "tile", odd_pairs("tile"))
    from_a = lax.ppermute(to_a, "tile", even_pairs("tile"))

    base, low_in = call(inner_kernel, (kept, inner_low), rho, vr, va, scratch=[pltpu.VMEM(rho.shape, F32)])
    parts_in = gather_bins(low_in)

    adv, low_out, sums = call(
        outer_kernel, (kept, outer_low, pltpu.VMEM((3, rows, cells), F32)), scal, rho, vr, va, base, from_a, from_b,
        scratch=[pltpu.VMEM((3, bins, cells), F32)] * 2, scalars=1,
    )
    parts_out = gather_direct(low_out)

    step, last = 1, lax.axis_size("bin") // 2
    others = lax.ppermute(sums, "bin", xor_pairs("bin", step))
    while step < last:
        step *= 2
        sums = sums + others
        others = lax.ppermute(sums, "bin", xor_pairs("bin", step))
    vr_out, va_out, gvr_out, gva_out = call(
        drag_kernel, (field, field, struct(gas.shape), struct(gas.shape)),
        scal, sums, others, gas, gvr, gva, vr, va, scalars=1,
    )

    gain_in = call(
        inner_gain_kernel, pltpu.VMEM((inner_rows, bins, cells), F32), coef_rows, *parts_in,
        scratch=[pltpu.VMEM((inner_rows, total, cells), BF16)],
    )
    density_out = call(
        outer_gain_kernel, field, coef_rows, adv, gain_in, *parts_out,
        scratch=[pltpu.VMEM((outer_rows, total, cells), BF16), pltpu.VMEM((outer_rows, bins, cells), F32)],
    )
    return density_out, vr_out, va_out, gvr_out, gva_out


def solution(mesh):
    field, flat = P("bin", "tile", None), P("tile", None)
    return jax.shard_map(
        body,
        mesh=mesh,
        in_specs=(field, field, field, flat, flat, flat, P("bin"), P("bin", None, None)),
        out_specs=(field, field, field, flat, flat),
        check_vma=False,
    )
```

```python
import functools

import jax
import jax.numpy as jnp
from jax import lax
from jax.experimental import pallas as pl
from jax.experimental.pallas import tpu as pltpu
from jax.sharding import PartitionSpec as P

COURANT = 0.2
COAGULATION = 0.5
HALO = 2
F32 = jnp.float32
BF16 = jnp.bfloat16

VMEM = pl.BlockSpec(memory_space=pltpu.VMEM)
ANY = pl.BlockSpec(memory_space=pl.ANY)


def minmod(a, b):
    return jnp.maximum(jnp.minimum(a, b), 0.0) + jnp.minimum(jnp.maximum(a, b), 0.0)


def face_flux(low, low_slope, high, high_slope, u):
    cu = COURANT * u
    left = low + (0.5 - 0.5 * cu) * low_slope
    right = high - (0.5 + 0.5 * cu) * high_slope
    return jnp.maximum(u, 0.0) * left + jnp.minimum(u, 0.0) * right


def shift(x, by, axis):
    return pltpu.roll(x, by % x.shape[axis], axis)


def load_kernel(rho_in, vr_in, va_in, stop_in, to_a_ref, to_b_ref, rho_ref, vr_ref, va_ref, table_ref, stop_ref, stop_sem, sems):
    bins, rows, cells = rho_ref.shape
    pieces = sems.shape[1]
    part = bins // pieces
    stop_copy = pltpu.make_async_copy(stop_in, stop_ref, stop_sem)
    stop_copy.start()
    copies = []
    for f, (source, target) in enumerate(((rho_in, rho_ref), (vr_in, vr_ref), (va_in, va_ref))):
        for p in range(pieces):
            at = pl.ds(p * part, part)
            copies.append(pltpu.make_async_copy(source.at[at], target.at[at], sems.at[f, p]))
    for copy in copies:
        copy.start()
    stop_copy.wait()
    square = (bins, bins)
    own = lax.broadcasted_iota(jnp.int32, square, 0) == lax.broadcasted_iota(jnp.int32, square, 1)
    stop = jnp.sum(jnp.where(own, jnp.broadcast_to(stop_ref[...], square), 0.0), axis=1, keepdims=True)
    rate = 1.0 / stop
    scale = 1.0 / (1.0 + rate)
    table_ref[0] = jnp.broadcast_to(rate * scale, (bins, cells))
    table_ref[1] = jnp.broadcast_to(scale, (bins, cells))
    for copy in copies[:2 * pieces]:
        copy.wait()
    even = lax.axis_index("tile") % 2 == 0
    up = (rho_ref[:, 0, :], rho_ref[:, 1, :], vr_ref[:, 0, :])
    down = (rho_ref[:, rows - 1, :], rho_ref[:, rows - 2, :], vr_ref[:, rows - 1, :])
    for n in range(3):
        to_a_ref[n] = jnp.where(even, down[n], up[n]).astype(BF16)
        to_b_ref[n] = jnp.where(even, up[n], down[n]).astype(BF16)
    for copy in copies[2 * pieces:]:
        copy.wait()


def radial(q, v, top, bottom):
    rows = q.shape[0]
    row = lax.broadcasted_iota(jnp.int32, q.shape, 0)
    first, last = row == 0, row == rows - 1
    q_next = jnp.where(last, bottom[0], shift(q, -1, 0))
    q_prev = jnp.where(first, top[0], shift(q, 1, 0))
    v_next = jnp.where(last, bottom[2], shift(v, -1, 0))
    v_prev = jnp.where(first, top[2], shift(v, 1, 0))
    d_next = q_next - q
    d_prev = q - q_prev
    s = minmod(d_prev, d_next)
    s_top = minmod(top[0] - top[1], d_prev)
    s_bottom = minmod(d_next, bottom[1] - bottom[0])
    s_prev = jnp.where(first, s_top, shift(s, 1, 0))
    s_next = jnp.where(last, s_bottom, shift(s, -1, 0))
    out = face_flux(q, s, q_next, s_next, 0.5 * (v + v_next))
    into = face_flux(q_prev, s_prev, q, s, 0.5 * (v_prev + v))
    return out - into


def azimuthal(q, v):
    q_next = shift(q, -1, 1)
    d = q_next - q
    s = minmod(shift(d, 1, 1), d)
    flux = face_flux(q, s, q_next, shift(s, -1, 1), 0.5 * (v + shift(v, -1, 1)))
    return flux - shift(flux, 1, 1)


def inner_rows(rows):
    return list(range(HALO, rows - HALO))


def outer_rows(rows):
    return list(range(HALO)) + list(range(rows - HALO, rows))


def lines_of(bins, picked):
    return (bins + 6) * len(picked)


def write_message(ref, start, picked, adv_ref, sums, halves_ref):
    bins, count = adv_ref.shape[0], len(picked)
    for n, r in enumerate(picked):
        ref[start + n * bins:start + (n + 1) * bins, :] = adv_ref[:, r, :].astype(BF16)
    for n in range(3):
        high = sums[n].astype(BF16).astype(F32)
        for half, value in enumerate((high, sums[n] - high)):
            for m, r in enumerate(picked):
                at = (2 * n + half) * count + m
                halves_ref[at:at + 1, :] = value[r:r + 1, :]
    ref[start + count * bins:start + lines_of(bins, picked), :] = halves_ref[...].astype(BF16)


def read_sums(ref, start, picked, bins, halves_ref, sums_ref):
    count = len(picked)
    halves_ref[...] = ref[start + count * bins:start + lines_of(bins, picked), :].astype(F32)
    for n in range(3):
        for m, r in enumerate(picked):
            high, low = 2 * n * count + m, (2 * n + 1) * count + m
            sums_ref[n, r:r + 1, :] = halves_ref[high:high + 1, :] + halves_ref[low:low + 1, :]


def weighed(sums, adv, vr, va, coupling):
    weight = adv * coupling
    return (sums[0] + weight * vr, sums[1] + weight * va, sums[2] + weight)


def inner_kernel(table_ref, rho_ref, vr_ref, va_ref, base_ref, message_ref, adv_ref, halves_ref):
    bins, rows, cells = rho_ref.shape
    zero = jnp.zeros((rows, cells), F32)
    none = (zero, zero, zero)
    sums = none
    for b in range(bins):
        q, vr, va = rho_ref[b], vr_ref[b], va_ref[b]
        base = q - COURANT * azimuthal(q, va)
        base_ref[b] = base
        adv = base - COURANT * radial(q, vr, none, none)
        adv_ref[b] = adv
        sums = weighed(sums, adv, vr, va, jnp.broadcast_to(table_ref[0, b:b + 1, :], q.shape))
    write_message(message_ref, 0, inner_rows(rows), adv_ref, sums, halves_ref)


def outer_kernel(table_ref, rho_ref, vr_ref, va_ref, base_ref, from_a_ref, from_b_ref, inner_ref, adv_ref, message_ref, both_ref, top_ref, bottom_ref, halves_ref):
    bins, rows, cells = rho_ref.shape
    tile, tiles = lax.axis_index("tile"), lax.axis_size("tile")
    even = tile % 2 == 0
    has_top = jnp.where(tile > 0, 1.0, 0.0)
    has_bottom = jnp.where(tile < tiles - 1, 1.0, 0.0)
    for n in range(3):
        a, b = from_a_ref[n].astype(F32), from_b_ref[n].astype(F32)
        top_ref[n] = jnp.where(even, b, a) * has_top
        bottom_ref[n] = jnp.where(even, a, b) * has_bottom
    shape = (rows, cells)
    zero = jnp.zeros(shape, F32)
    sums = (zero, zero, zero)
    for b in range(bins):
        top = tuple(jnp.broadcast_to(top_ref[n, b:b + 1, :], shape) for n in range(3))
        bottom = tuple(jnp.broadcast_to(bottom_ref[n, b:b + 1, :], shape) for n in range(3))
        vr = vr_ref[b]
        adv = base_ref[b] - COURANT * radial(rho_ref[b], vr, top, bottom)
        adv_ref[b] = adv
        sums = weighed(sums, adv, vr, va_ref[b], jnp.broadcast_to(table_ref[0, b:b + 1, :], shape))
    write_message(message_ref, 0, outer_rows(rows), adv_ref, sums, halves_ref)
    split = inner_ref.shape[0]
    both_ref[:split, :] = inner_ref[...]
    both_ref[split:, :] = message_ref[...]


def total_sums(at, offset, bit):
    if bit == 0:
        return at(offset)
    return total_sums(at, offset, bit // 2) + total_sums(at, offset ^ bit, bit // 2)


def drag_kernel(layout, table_ref, gas_ref, gvr_ref, gva_ref, vr_ref, va_ref, *refs):
    bins, rows, _ = vr_ref.shape
    count = len(layout[0])
    messages, (vr_out, va_out, gvr_out, gva_out, sums_ref, halves_in_ref, halves_out_ref) = refs[:-7], refs[-7:]
    for offset in range(count):
        for places, picked, halves_ref in ((layout[0], inner_rows(rows), halves_in_ref), (layout[1], outer_rows(rows), halves_out_ref)):
            which, start = places[offset]
            read_sums(messages[which], start, picked, bins, halves_ref, sums_ref.at[offset])
    sums = [total_sums(lambda o, n=n: sums_ref[o, n], 0, count // 2) for n in range(3)]
    gas = gas_ref[...]
    denom = gas + sums[2]
    new_r = (gas * gvr_ref[...] + sums[0]) / denom
    new_a = (gas * gva_ref[...] + sums[1]) / denom
    gvr_out[...] = new_r
    gva_out[...] = new_a
    for b in range(bins):
        coupling = jnp.broadcast_to(table_ref[0, b:b + 1, :], gas.shape)
        scale = jnp.broadcast_to(table_ref[1, b:b + 1, :], gas.shape)
        vr_out[b] = vr_ref[b] * scale + coupling * new_r
        va_out[b] = va_ref[b] * scale + coupling * new_a


def gather_low(places, messages, dens_ref, bins):
    here = lax.axis_index("bin")
    for offset, (which, start) in enumerate(places):
        at = pl.multiple_of((here ^ offset) * bins, bins)
        for n in range(dens_ref.shape[0]):
            dens_ref[n, pl.ds(at, bins), :] = messages[which][start + n * bins:start + (n + 1) * bins, :]


def gain_rows(coef_ref, dens_ref, gain_ref, bins, n_rows):
    total = dens_ref.shape[1]
    group = 8

    def one_row(n, carry):
        low = dens_ref[n]
        wide = low.astype(F32)
        acc = jnp.zeros((bins, low.shape[1]), F32)
        for i in range(0, total, group):
            inner = jnp.dot(coef_ref[i * bins:(i + group) * bins, :], low, preferred_element_type=F32)
            for g in range(group):
                acc = acc + inner[g * bins:(g + 1) * bins] * wide[i + g:i + g + 1]
        gain_ref[n] = acc
        return carry

    lax.fori_loop(0, n_rows, one_row, 0)


def inner_gain_kernel(places, coef_ref, *refs):
    messages, (gain_ref, dens_ref) = refs[:-2], refs[-2:]
    n_rows, bins, _ = gain_ref.shape
    gather_low(places, messages, dens_ref, bins)
    gain_rows(coef_ref, dens_ref, gain_ref, bins, n_rows)


def outer_gain_kernel(places, after_ref, coef_ref, adv_ref, inner_ref, *refs):
    del after_ref
    messages, (out_ref, dens_ref, gain_ref) = refs[:-3], refs[-3:]
    bins, rows, _ = adv_ref.shape
    picked = outer_rows(rows)
    gather_low(places, messages, dens_ref, bins)
    gain_rows(coef_ref, dens_ref, gain_ref, bins, len(picked))
    for n, r in enumerate(picked):
        out_ref[:, r, :] = adv_ref[:, r, :] + COAGULATION * gain_ref[n]
    for n, r in enumerate(inner_rows(rows)):
        out_ref[:, r, :] = adv_ref[:, r, :] + COAGULATION * inner_ref[n]


def struct(shape, dtype=F32):
    return jax.ShapeDtypeStruct(shape, dtype)


def call(kernel, outs, *args, scratch=(), remote=()):
    specs = [ANY if n in remote else VMEM for n in range(len(args))]
    placed = [x if n in remote else pltpu.with_memory_space_constraint(x, pltpu.VMEM) for n, x in enumerate(args)]
    return pl.pallas_call(
        kernel,
        out_shape=outs,
        in_specs=specs,
        out_specs=jax.tree.map(lambda _: VMEM, outs, is_leaf=lambda x: hasattr(x, "dtype")),
        scratch_shapes=scratch,
    )(*placed)


def xor_pairs(axis, bit):
    return [(i, i ^ bit) for i in range(lax.axis_size(axis))]


def even_pairs(axis):
    return xor_pairs(axis, 1)


def odd_pairs(axis):
    count = lax.axis_size(axis)
    pairs = [(0, count - 1), (count - 1, 0)]
    for i in range(1, count - 1, 2):
        pairs += [(i, i + 1), (i + 1, i)]
    return pairs


def body(rho, vr, va, gas, gvr, gva, stop_time, coef):
    bins, rows, cells = rho.shape
    total = coef.shape[1]
    inner, outer = inner_rows(rows), outer_rows(rows)
    coef_rows = jnp.transpose(coef, (1, 0, 2)).reshape(total * bins, total)
    field, kept = struct(rho.shape), pltpu.VMEM(rho.shape, F32)
    flat = struct(gas.shape)
    halo = pltpu.VMEM((3, bins, cells), BF16)
    inner_lines, outer_lines = lines_of(bins, inner), lines_of(bins, outer)
    halves_in, halves_out = (pltpu.VMEM((6 * len(picked), cells), F32) for picked in (inner, outer))

    pieces = 2
    to_a, to_b, rho, vr, va, table = call(
        load_kernel, (halo, halo, kept, kept, kept, pltpu.VMEM((2, bins, cells), F32)), rho, vr, va, stop_time[None],
        scratch=[pltpu.VMEM((1, bins), F32), pltpu.SemaphoreType.DMA, pltpu.SemaphoreType.DMA((3, pieces))],
        remote=(0, 1, 2, 3),
    )
    from_b = lax.ppermute(to_b, "tile", odd_pairs("tile"))
    from_a = lax.ppermute(to_a, "tile", even_pairs("tile"))

    groups = lax.axis_size("bin")
    half = groups // 2
    base, low_in = call(
        inner_kernel, (kept, pltpu.VMEM((inner_lines, cells), BF16)), table, rho, vr, va, scratch=[kept, halves_in],
    )
    far_in = lax.ppermute(low_in, "bin", xor_pairs("bin", half))

    adv, low_out, low_all = call(
        outer_kernel, (kept, pltpu.VMEM((outer_lines, cells), BF16), pltpu.VMEM((inner_lines + outer_lines, cells), BF16)),
        table, rho, vr, va, base, from_a, from_b, low_in,
        scratch=[pltpu.VMEM((3, bins, cells), F32)] * 2 + [halves_out],
    )
    far_out = [lax.ppermute(low_out, "bin", xor_pairs("bin", at)) for at in range(groups - 1, half - 1, -1)][::-1]
    near_all = [lax.ppermute(low_all, "bin", xor_pairs("bin", at)) for at in range(1, half)]
    passed_in = [lax.ppermute(far_in, "bin", xor_pairs("bin", at)) for at in range(1, half)]

    in_messages = [low_in] + near_all + [far_in] + passed_in
    in_places = [(n, 0) for n in range(groups)]
    out_messages = [low_out] + near_all + far_out
    out_places = [(n, inner_lines if 0 < n < half else 0) for n in range(groups)]
    drag_out = [(n if 0 < n < half else groups + (n - half + 1 if n else 0), start) for n, start in out_places]
    drag_messages = in_messages + [low_out] + far_out

    gain_in = call(
        functools.partial(inner_gain_kernel, in_places), pltpu.VMEM((len(inner), bins, cells), F32), coef_rows, *in_messages,
        scratch=[pltpu.VMEM((len(inner), total, cells), BF16)],
    )
    vr_out, va_out, gvr_out, gva_out = call(
        functools.partial(drag_kernel, (in_places, drag_out)), (field, field, flat, flat),
        table, gas, gvr, gva, vr, va, *drag_messages,
        scratch=[pltpu.VMEM((groups, 3, rows, cells), F32), halves_in, halves_out],
    )
    density_out = call(
        functools.partial(outer_gain_kernel, out_places), field, gvr_out, coef_rows, adv, gain_in, *out_messages,
        scratch=[pltpu.VMEM((len(outer), total, cells), BF16), pltpu.VMEM((len(outer), bins, cells), F32)],
        remote=(0,),
    )
    return density_out, vr_out, va_out, gvr_out, gva_out


def solution(mesh):
    field, flat = P("bin", "tile", None), P("tile", None)
    return jax.shard_map(
        body,
        mesh=mesh,
        in_specs=(field, field, field, flat, flat, flat, P("bin"), P("bin", None, None)),
        out_specs=(field, field, field, flat, flat),
        check_vma=False,
    )
```

```python
import functools

import jax
import jax.numpy as jnp
from jax import lax
from jax.experimental import pallas as pl
from jax.experimental.pallas import tpu as pltpu
from jax.sharding import PartitionSpec as P


COURANT = 0.2
COAGULATION = 0.5
HALO = 2
SMALL_BYTES = 2**19
F32 = jnp.float32
BF16 = jnp.bfloat16

VMEM = pl.BlockSpec(memory_space=pltpu.VMEM)
ANY = pl.BlockSpec(memory_space=pl.ANY)


def minmod(a, b):
    return jnp.maximum(jnp.minimum(a, b), 0.0) + jnp.minimum(jnp.maximum(a, b), 0.0)


def face_flux(low, low_slope, high, high_slope, u):
    cu = COURANT * u
    left = low + (0.5 - 0.5 * cu) * low_slope
    right = high - (0.5 + 0.5 * cu) * high_slope
    return jnp.maximum(u, 0.0) * left + jnp.minimum(u, 0.0) * right


def shift(x, by, axis):
    return pltpu.roll(x, by % x.shape[axis], axis)


def load_kernel(rho_in, vr_in, va_in, stop_in, to_a_ref, to_b_ref, rho_ref, vr_ref, va_ref, table_ref, stop_ref, stop_sem, sems):
    bins, rows, cells = rho_ref.shape
    pieces = sems.shape[1]
    part = bins // pieces
    stop_copy = pltpu.make_async_copy(stop_in, stop_ref, stop_sem)
    stop_copy.start()
    copies = []
    for f, (source, target) in enumerate(((rho_in, rho_ref), (vr_in, vr_ref), (va_in, va_ref))):
        for p in range(pieces):
            at = pl.ds(p * part, part)
            copies.append(pltpu.make_async_copy(source.at[at], target.at[at], sems.at[f, p]))
    for copy in copies:
        copy.start()
    stop_copy.wait()
    square = (bins, bins)
    own = lax.broadcasted_iota(jnp.int32, square, 0) == lax.broadcasted_iota(jnp.int32, square, 1)
    stop = jnp.sum(jnp.where(own, jnp.broadcast_to(stop_ref[...], square), 0.0), axis=1, keepdims=True)
    rate = 1.0 / stop
    scale = 1.0 / (1.0 + rate)
    table_ref[0] = jnp.broadcast_to(rate * scale, (bins, cells))
    table_ref[1] = jnp.broadcast_to(scale, (bins, cells))
    for copy in copies[:2 * pieces]:
        copy.wait()
    even = lax.axis_index("tile") % 2 == 0
    up = (rho_ref[:, 0, :], rho_ref[:, 1, :], vr_ref[:, 0, :])
    down = (rho_ref[:, rows - 1, :], rho_ref[:, rows - 2, :], vr_ref[:, rows - 1, :])
    for n in range(3):
        to_a_ref[n] = jnp.where(even, down[n], up[n]).astype(BF16)
        to_b_ref[n] = jnp.where(even, up[n], down[n]).astype(BF16)
    for copy in copies[2 * pieces:]:
        copy.wait()


def radial(q, v, top, bottom):
    rows = q.shape[0]
    row = lax.broadcasted_iota(jnp.int32, q.shape, 0)
    first, last = row == 0, row == rows - 1
    q_next = jnp.where(last, bottom[0], shift(q, -1, 0))
    q_prev = jnp.where(first, top[0], shift(q, 1, 0))
    v_next = jnp.where(last, bottom[2], shift(v, -1, 0))
    v_prev = jnp.where(first, top[2], shift(v, 1, 0))
    d_next = q_next - q
    d_prev = q - q_prev
    s = minmod(d_prev, d_next)
    s_top = minmod(top[0] - top[1], d_prev)
    s_bottom = minmod(d_next, bottom[1] - bottom[0])
    s_prev = jnp.where(first, s_top, shift(s, 1, 0))
    s_next = jnp.where(last, s_bottom, shift(s, -1, 0))
    out = face_flux(q, s, q_next, s_next, 0.5 * (v + v_next))
    into = face_flux(q_prev, s_prev, q, s, 0.5 * (v_prev + v))
    return out - into


def azimuthal(q, v):
    q_next = shift(q, -1, 1)
    d = q_next - q
    s = minmod(shift(d, 1, 1), d)
    flux = face_flux(q, s, q_next, shift(s, -1, 1), 0.5 * (v + shift(v, -1, 1)))
    return flux - shift(flux, 1, 1)


def inner_rows(rows):
    return list(range(HALO, rows - HALO))


def outer_rows(rows):
    return list(range(HALO)) + list(range(rows - HALO, rows))


def lines_of(bins, picked):
    return (bins + 6) * len(picked)


def write_message(ref, start, picked, adv_ref, sums, halves_ref):
    bins, count = adv_ref.shape[0], len(picked)
    for n, r in enumerate(picked):
        ref[start + n * bins:start + (n + 1) * bins, :] = adv_ref[:, r, :].astype(BF16)
    for n in range(3):
        high = sums[n].astype(BF16).astype(F32)
        for half, value in enumerate((high, sums[n] - high)):
            for m, r in enumerate(picked):
                at = (2 * n + half) * count + m
                halves_ref[at:at + 1, :] = value[r:r + 1, :]
    ref[start + count * bins:start + lines_of(bins, picked), :] = halves_ref[...].astype(BF16)


def read_sums(ref, start, picked, bins, halves_ref, sums_ref):
    count = len(picked)
    halves_ref[...] = ref[start + count * bins:start + lines_of(bins, picked), :].astype(F32)
    for n in range(3):
        for m, r in enumerate(picked):
            high, low = 2 * n * count + m, (2 * n + 1) * count + m
            sums_ref[n, r:r + 1, :] = halves_ref[high:high + 1, :] + halves_ref[low:low + 1, :]


def weighed(sums, adv, vr, va, coupling):
    weight = adv * coupling
    return (sums[0] + weight * vr, sums[1] + weight * va, sums[2] + weight)


def inner_kernel(table_ref, rho_ref, vr_ref, va_ref, base_ref, message_ref, adv_ref, halves_ref):
    bins, rows, cells = rho_ref.shape
    zero = jnp.zeros((rows, cells), F32)
    none = (zero, zero, zero)
    sums = none
    for b in range(bins):
        q, vr, va = rho_ref[b], vr_ref[b], va_ref[b]
        base = q - COURANT * azimuthal(q, va)
        base_ref[b] = base
        adv = base - COURANT * radial(q, vr, none, none)
        adv_ref[b] = adv
        sums = weighed(sums, adv, vr, va, jnp.broadcast_to(table_ref[0, b:b + 1, :], q.shape))
    write_message(message_ref, 0, inner_rows(rows), adv_ref, sums, halves_ref)


def outer_kernel(table_ref, rho_ref, vr_ref, va_ref, base_ref, from_a_ref, from_b_ref, inner_ref, adv_ref, message_ref, both_ref, top_ref, bottom_ref, halves_ref):
    bins, rows, cells = rho_ref.shape
    tile, tiles = lax.axis_index("tile"), lax.axis_size("tile")
    even = tile % 2 == 0
    has_top = jnp.where(tile > 0, 1.0, 0.0)
    has_bottom = jnp.where(tile < tiles - 1, 1.0, 0.0)
    for n in range(3):
        a, b = from_a_ref[n].astype(F32), from_b_ref[n].astype(F32)
        top_ref[n] = jnp.where(even, b, a) * has_top
        bottom_ref[n] = jnp.where(even, a, b) * has_bottom
    shape = (rows, cells)
    zero = jnp.zeros(shape, F32)
    sums = (zero, zero, zero)
    for b in range(bins):
        top = tuple(jnp.broadcast_to(top_ref[n, b:b + 1, :], shape) for n in range(3))
        bottom = tuple(jnp.broadcast_to(bottom_ref[n, b:b + 1, :], shape) for n in range(3))
        vr = vr_ref[b]
        adv = base_ref[b] - COURANT * radial(rho_ref[b], vr, top, bottom)
        adv_ref[b] = adv
        sums = weighed(sums, adv, vr, va_ref[b], jnp.broadcast_to(table_ref[0, b:b + 1, :], shape))
    write_message(message_ref, 0, outer_rows(rows), adv_ref, sums, halves_ref)
    split = inner_ref.shape[0]
    both_ref[:split, :] = inner_ref[...]
    both_ref[split:, :] = message_ref[...]


def total_sums(at, offset, bit):
    if bit == 0:
        return at(offset)
    return total_sums(at, offset, bit // 2) + total_sums(at, offset ^ bit, bit // 2)


def drag(layout, table_ref, gas_ref, gvr_ref, gva_ref, vr_ref, va_ref, messages, vr_out, va_out, gvr_out, gva_out, sums_ref, halves_in_ref, halves_out_ref):
    bins, rows, _ = vr_ref.shape
    count = len(layout[0])
    for offset in range(count):
        for places, picked, halves_ref in ((layout[0], inner_rows(rows), halves_in_ref), (layout[1], outer_rows(rows), halves_out_ref)):
            which, start = places[offset]
            read_sums(messages[which], start, picked, bins, halves_ref, sums_ref.at[offset])
    sums = [total_sums(lambda o, n=n: sums_ref[o, n], 0, count // 2) for n in range(3)]
    gas = gas_ref[...]
    denom = gas + sums[2]
    new_r = (gas * gvr_ref[...] + sums[0]) / denom
    new_a = (gas * gva_ref[...] + sums[1]) / denom
    gvr_out[...] = new_r
    gva_out[...] = new_a
    for b in range(bins):
        coupling = jnp.broadcast_to(table_ref[0, b:b + 1, :], gas.shape)
        scale = jnp.broadcast_to(table_ref[1, b:b + 1, :], gas.shape)
        vr_out[b] = vr_ref[b] * scale + coupling * new_r
        va_out[b] = va_ref[b] * scale + coupling * new_a


def weights_kernel(rows_ref, swapped_ref, out_ref):
    lines, total = rows_ref.shape
    bins = lines // total
    here = lax.axis_index("bin")
    shift_of = (bins - 1).bit_length()
    taker = lax.shift_right_logical(lax.broadcasted_iota(jnp.int32, (lines, total), 0), 2 * shift_of) ^ here
    giver = lax.shift_right_logical(lax.broadcasted_iota(jnp.int32, (lines, total), 1), shift_of) ^ here
    one = rows_ref[...].astype(F32)
    both = one + swapped_ref[...].astype(F32)
    high = both.astype(BF16).astype(F32)
    earlier = giver < taker
    zero = jnp.zeros_like(one)
    out_ref[:, :total] = jnp.where(giver == taker, one, jnp.where(earlier, high, zero)).astype(BF16)
    out_ref[:, total:] = jnp.where(earlier, both - high, zero).astype(BF16)


def block_start(offset, bins):
    return pl.multiple_of((lax.axis_index("bin") ^ offset) * bins, bins)


def add_blocks(weights_ref, messages, places, first, last, dens_ref, gain_ref, old_ref):
    n_rows, bins, cells = gain_ref.shape
    total = dens_ref.shape[1] // 2
    group = 8
    for offset in range(len(places)):
        at = block_start(offset, bins)
        for n in range(n_rows):
            if offset < last:
                which, start = places[offset]
                low = messages[which][start + n * bins:start + (n + 1) * bins, :]
            else:
                low = jnp.zeros((bins, cells), BF16)
            dens_ref[n, pl.ds(at, bins), :] = low
            dens_ref[n, pl.ds(total + at, bins), :] = low
    for n in range(n_rows):
        both = dens_ref[n]
        acc = jnp.zeros((bins, cells), F32) if old_ref is None else old_ref[n]
        for offset in range(first, last):
            which, start = places[offset]
            wide = messages[which][start + n * bins:start + (n + 1) * bins, :].astype(F32)
            at = block_start(offset, bins) * bins
            for i in range(0, bins, group):
                lines = pl.ds(pl.multiple_of(at + i * bins, group * bins), group * bins)
                inner = jnp.dot(weights_ref[lines, :], both, preferred_element_type=F32)
                for g in range(group):
                    acc = acc + inner[g * bins:(g + 1) * bins] * wide[i + g:i + g + 1]
        gain_ref[n] = acc


def first_gain_kernel(in_places, out_places, weights_ref, *refs):
    messages, (gain_in_ref, gain_out_ref, dens_in_ref, dens_out_ref) = refs[:-4], refs[-4:]
    half = len(in_places) // 2
    add_blocks(weights_ref, messages, out_places, 0, half, dens_out_ref, gain_out_ref, None)
    add_blocks(weights_ref, messages, in_places, 0, half + 1, dens_in_ref, gain_in_ref, None)


def last_kernel(
    in_places, out_places, table_ref, gas_ref, gvr_ref, gva_ref, vr_ref, va_ref, weights_ref, adv_ref, gain_in_ref, gain_out_ref, *refs
):
    messages, refs = refs[:-18], refs[-18:]
    outs, kept, refs = refs[:5], refs[5:10], refs[10:]
    new_in_ref, new_out_ref, dens_in_ref, dens_out_ref, sums_ref, halves_in_ref, halves_out_ref, sems = refs
    _, rows, _ = adv_ref.shape
    count = len(in_places)
    copies = [pltpu.make_async_copy(kept[n], outs[n], sems.at[n]) for n in range(5)]
    density_ref, vr_out, va_out, gvr_out, gva_out = kept
    drag(
        (in_places, out_places), table_ref, gas_ref, gvr_ref, gva_ref, vr_ref, va_ref, messages,
        vr_out, va_out, gvr_out, gva_out, sums_ref, halves_in_ref, halves_out_ref,
    )
    for copy in copies[1:]:
        copy.start()
    add_blocks(weights_ref, messages, in_places, count // 2 + 1, count, dens_in_ref, new_in_ref, gain_in_ref)
    for n, r in enumerate(inner_rows(rows)):
        density_ref[:, r, :] = adv_ref[:, r, :] + COAGULATION * new_in_ref[n]
    add_blocks(weights_ref, messages, out_places, count // 2, count, dens_out_ref, new_out_ref, gain_out_ref)
    for n, r in enumerate(outer_rows(rows)):
        density_ref[:, r, :] = adv_ref[:, r, :] + COAGULATION * new_out_ref[n]
    copies[0].start()
    for copy in copies:
        copy.wait()


def struct(shape, dtype=F32):
    return jax.ShapeDtypeStruct(shape, dtype)


def call(kernel, outs, *args, scratch=(), remote=(), loose=(), spec=VMEM):
    specs = [ANY if n in remote else VMEM for n in range(len(args))]
    placed = [x if n in remote or n in loose else pltpu.with_memory_space_constraint(x, pltpu.VMEM) for n, x in enumerate(args)]
    return pl.pallas_call(
        kernel,
        out_shape=outs,
        in_specs=specs,
        out_specs=jax.tree.map(lambda _: spec, outs, is_leaf=lambda x: hasattr(x, "dtype")),
        scratch_shapes=scratch,
    )(*placed)


def xor_pairs(axis, bit):
    return [(i, i ^ bit) for i in range(lax.axis_size(axis))]


def even_pairs(axis):
    return xor_pairs(axis, 1)


def odd_pairs(axis):
    count = lax.axis_size(axis)
    pairs = [(0, count - 1), (count - 1, 0)]
    for i in range(1, count - 1, 2):
        pairs += [(i, i + 1), (i + 1, i)]
    return pairs


def body(rho, vr, va, gas, gvr, gva, stop_time, coef):
    bins, rows, cells = rho.shape
    total = coef.shape[1]
    inner, outer = inner_rows(rows), outer_rows(rows)
    weights_size = (total * bins, 2 * total)
    small = 2 * weights_size[0] * weights_size[1] <= SMALL_BYTES
    weights = call(
        weights_kernel, (pltpu.VMEM if small else struct)(weights_size, BF16),
        jnp.transpose(coef, (1, 0, 2)).reshape(total * bins, total), jnp.transpose(coef, (2, 0, 1)).reshape(total * bins, total),
    )
    field, kept = struct(rho.shape), pltpu.VMEM(rho.shape, F32)
    flat = struct(gas.shape)
    halo = pltpu.VMEM((3, bins, cells), BF16)
    inner_lines, outer_lines = lines_of(bins, inner), lines_of(bins, outer)
    halves_in, halves_out = (pltpu.VMEM((6 * len(picked), cells), F32) for picked in (inner, outer))

    pieces = 2
    to_a, to_b, rho, vr, va, table = call(
        load_kernel, (halo, halo, kept, kept, kept, pltpu.VMEM((2, bins, cells), F32)), rho, vr, va, stop_time[None],
        scratch=[pltpu.VMEM((1, bins), F32), pltpu.SemaphoreType.DMA, pltpu.SemaphoreType.DMA((3, pieces))],
        remote=(0, 1, 2, 3),
    )
    from_b = lax.ppermute(to_b, "tile", odd_pairs("tile"))
    from_a = lax.ppermute(to_a, "tile", even_pairs("tile"))

    groups = lax.axis_size("bin")
    half = groups // 2
    base, low_in = call(
        inner_kernel, (kept, pltpu.VMEM((inner_lines, cells), BF16)), table, rho, vr, va,
        scratch=[kept, halves_in],
    )
    far_in = lax.ppermute(low_in, "bin", xor_pairs("bin", half))

    adv, low_out, low_all = call(
        outer_kernel, (kept, pltpu.VMEM((outer_lines, cells), BF16), pltpu.VMEM((inner_lines + outer_lines, cells), BF16)),
        table, rho, vr, va, base, from_a, from_b, low_in,
        scratch=[pltpu.VMEM((3, bins, cells), F32)] * 2 + [halves_out],
    )
    far_out = [lax.ppermute(low_out, "bin", xor_pairs("bin", at)) for at in range(groups - 1, half - 1, -1)][::-1]
    near_all = [lax.ppermute(low_all, "bin", xor_pairs("bin", at)) for at in range(1, half)]
    passed_in = [lax.ppermute(far_in, "bin", xor_pairs("bin", at)) for at in range(1, half)]

    messages = [low_in] + near_all + [far_in] + passed_in + [low_out] + far_out
    in_places = [(n, 0) for n in range(groups)]
    out_places = [(n, inner_lines) if 0 < n < half else (groups + (n - half + 1 if n else 0), 0) for n in range(groups)]

    ready = half + 1
    gains = [pltpu.VMEM((len(picked), bins, cells), F32) for picked in (inner, outer)]
    dens = [pltpu.VMEM((len(picked), 2 * total, cells), BF16) for picked in (inner, outer)]
    early = messages[:ready] + [low_out]
    early_out = [(n, inner_lines) if n else (ready, 0) for n in range(half)] + [None] * (groups - half)
    gain_in, gain_out = call(
        functools.partial(first_gain_kernel, in_places, early_out), tuple(gains), weights, *early, scratch=dens, loose=() if small else (0,),
    )
    return call(
        functools.partial(last_kernel, in_places, out_places), (field, field, field, flat, flat),
        table, gas, gvr, gva, vr, va, weights, adv, gain_in, gain_out, *messages,
        scratch=[kept] * 3 + [pltpu.VMEM(gas.shape, F32)] * 2 + gains + dens
        + [pltpu.VMEM((groups, 3, rows, cells), F32), halves_in, halves_out, pltpu.SemaphoreType.DMA((5,))],
        loose=() if small else (6,), spec=ANY,
    )


def solution(mesh):
    field, flat = P("bin", "tile", None), P("tile", None)
    return jax.shard_map(
        body,
        mesh=mesh,
        in_specs=(field, field, field, flat, flat, flat, P("bin"), P("bin", None, None)),
        out_specs=(field, field, field, flat, flat),
        check_vma=False,
    )
```

```python
import functools

import jax
import jax.numpy as jnp
from jax import lax
from jax.experimental import pallas as pl
from jax.experimental.pallas import tpu as pltpu
from jax.sharding import PartitionSpec as P


COURANT = 0.2
COAGULATION = 0.5
HALO = 2
SMALL_BYTES = 2**19
F32 = jnp.float32
BF16 = jnp.bfloat16

VMEM = pl.BlockSpec(memory_space=pltpu.VMEM)
ANY = pl.BlockSpec(memory_space=pl.ANY)


def minmod(a, b):
    return jnp.maximum(jnp.minimum(a, b), 0.0) + jnp.minimum(jnp.maximum(a, b), 0.0)


def face_flux(low, low_slope, high, high_slope, u):
    cu = COURANT * u
    left = low + (0.5 - 0.5 * cu) * low_slope
    right = high - (0.5 + 0.5 * cu) * high_slope
    return jnp.maximum(u, 0.0) * left + jnp.minimum(u, 0.0) * right


def shift(x, by, axis):
    return pltpu.roll(x, by % x.shape[axis], axis)


def edge_rows(rows, width):
    return list(range(width)) + list(range(rows - width, rows))


def load_kernel(rho_in, vr_in, va_in, stop_in, to_a_ref, to_b_ref, rho_ref, vr_ref, va_ref, table_ref, stop_ref, stop_sem, sems):
    _, bins, cells = rho_ref.shape
    rows = rho_in.shape[1]
    stop_copy = pltpu.make_async_copy(stop_in, stop_ref, stop_sem)
    copies = []
    for source, target in ((rho_in, rho_ref), (vr_in, vr_ref), (va_in, va_ref)):
        for n, r in enumerate(edge_rows(rows, target.shape[0] // 2)):
            copies.append(pltpu.make_async_copy(source.at[:, r, :], target.at[n], sems.at[len(copies)]))
    for copy in copies:
        copy.start()
    stop_copy.start()
    stop_copy.wait()
    square = (bins, bins)
    own = lax.broadcasted_iota(jnp.int32, square, 0) == lax.broadcasted_iota(jnp.int32, square, 1)
    stop = jnp.sum(jnp.where(own, jnp.broadcast_to(stop_ref[...], square), 0.0), axis=1, keepdims=True)
    rate = 1.0 / stop
    scale = 1.0 / (1.0 + rate)
    table_ref[0] = jnp.broadcast_to(rate * scale, (bins, cells))
    table_ref[1] = jnp.broadcast_to(scale, (bins, cells))
    for copy in copies:
        copy.wait()
    even = lax.axis_index("tile") % 2 == 0
    up = (rho_ref[0], rho_ref[1], vr_ref[0])
    last, last_v = rho_ref.shape[0] - 1, vr_ref.shape[0] - 1
    down = (rho_ref[last], rho_ref[last - 1], vr_ref[last_v])
    for n in range(3):
        to_a_ref[n] = jnp.where(even, down[n], up[n]).astype(BF16)
        to_b_ref[n] = jnp.where(even, up[n], down[n]).astype(BF16)


def radial_inside(q, v):
    rows = q.shape[0]
    row = lax.broadcasted_iota(jnp.int32, q.shape, 0)
    q_next = shift(q, -1, 0)
    d = q_next - q
    s = minmod(shift(d, 1, 0), d)
    flux = face_flux(q, s, q_next, shift(s, -1, 0), 0.5 * (v + shift(v, -1, 0)))
    flux = jnp.where((row >= HALO - 1) & (row < rows - HALO), flux, 0.0)
    return flux - shift(flux, 1, 0)


def azimuthal(q, v):
    q_next = shift(q, -1, 1)
    d = q_next - q
    s = minmod(shift(d, 1, 1), d)
    flux = face_flux(q, s, q_next, shift(s, -1, 1), 0.5 * (v + shift(v, -1, 1)))
    return flux - shift(flux, 1, 1)


def inner_rows(rows):
    return list(range(HALO, rows - HALO))


def outer_rows(rows):
    return edge_rows(rows, HALO)


def lines_of(bins, picked):
    return (bins + 6) * len(picked)


def write_message(ref, densities, sums, halves_ref):
    bins, count = densities[0].shape[0], len(densities)
    for m in range(count):
        ref[m * bins:(m + 1) * bins, :] = densities[m].astype(BF16)
        for n in range(3):
            high = sums[n][m].astype(BF16).astype(F32)
            for half, value in enumerate((high, sums[n][m] - high)):
                at = (2 * n + half) * count + m
                halves_ref[at:at + 1, :] = value
    ref[count * bins:, :] = halves_ref[...].astype(BF16)


def read_sums(ref, picked, bins, halves_ref, sums_ref):
    count = len(picked)
    halves_ref[...] = ref[count * bins:, :].astype(F32)
    for n in range(3):
        for m, r in enumerate(picked):
            high, low = 2 * n * count + m, (2 * n + 1) * count + m
            sums_ref[n, r:r + 1, :] = halves_ref[high:high + 1, :] + halves_ref[low:low + 1, :]


def weighed(sums, adv, vr, va, coupling):
    weight = adv * coupling
    return (sums[0] + weight * vr, sums[1] + weight * va, sums[2] + weight)


def inner_kernel(table_ref, rho_ref, vr_ref, va_ref, message_ref, adv_ref, part_ref, all_ref, halves_ref):
    bins, rows, cells = rho_ref.shape
    zero = jnp.zeros((rows, cells), F32)
    sums = (zero, zero, zero)
    for b in range(bins):
        q, vr, va = rho_ref[b], vr_ref[b], va_ref[b]
        adv = q - COURANT * (azimuthal(q, va) + radial_inside(q, vr))
        all_ref[b] = adv
        sums = weighed(sums, adv, vr, va, jnp.broadcast_to(table_ref[0, b:b + 1, :], q.shape))
    picked = inner_rows(rows)
    densities = [all_ref[:, r, :] for r in picked]
    for n, density in enumerate(densities):
        adv_ref[n] = density
    write_message(message_ref, densities, [[x[r:r + 1] for r in picked] for x in sums], halves_ref)
    for n, r in enumerate(outer_rows(rows)):
        part_ref[n] = all_ref[:, r, :]


def outer_kernel(table_ref, rho_ref, vr_ref, va_ref, part_ref, from_a_ref, from_b_ref, adv_ref, message_ref, halves_ref):
    tile, tiles = lax.axis_index("tile"), lax.axis_size("tile")
    even = tile % 2 == 0
    has_top = jnp.where(tile > 0, 1.0, 0.0)
    has_bottom = jnp.where(tile < tiles - 1, 1.0, 0.0)
    top, bottom = [], []
    for n in range(3):
        a, b = from_a_ref[n].astype(F32), from_b_ref[n].astype(F32)
        top.append(jnp.where(even, b, a) * has_top)
        bottom.append(jnp.where(even, a, b) * has_bottom)

    def edge(nearest, nearest_part, v, sign, halo):
        q = [halo[1], halo[0]] + nearest
        d = [sign * (q[n] - q[n + 1]) for n in range(4)]
        s = [minmod(d[n], d[n + 1]) for n in range(3)]
        speed = [0.5 * (halo[2] + v[0]), 0.5 * (v[0] + v[1])]
        flux = []
        for n in range(2):
            low, high = (n, n + 1) if sign < 0 else (n + 1, n)
            flux.append(face_flux(q[low + 1], s[low], q[high + 1], s[high], speed[n]))
        outermost = nearest_part[0] - COURANT * sign * (flux[0] - flux[1])
        return outermost, nearest_part[1] - COURANT * sign * flux[1]

    row = [rho_ref[n] for n in range(rho_ref.shape[0])]
    speed = [vr_ref[n] for n in range(vr_ref.shape[0])]
    part = [part_ref[n] for n in range(part_ref.shape[0])]
    first, second = edge(row[:3], part[:2], speed[:2], -1.0, top)
    last, before = edge(row[:2:-1], part[:1:-1], speed[:1:-1], 1.0, bottom)
    densities = [first, second, before, last]
    sums = [[], [], []]
    for n, density in enumerate(densities):
        adv_ref[n] = density
        weight = density * table_ref[0]
        for kind, value in enumerate((weight * speed[n], weight * va_ref[n], weight)):
            sums[kind].append(jnp.sum(value, axis=0, keepdims=True))
    write_message(message_ref, densities, sums, halves_ref)


def total_sums(at, offset, bit):
    if bit == 0:
        return at(offset)
    return total_sums(at, offset, bit // 2) + total_sums(at, offset ^ bit, bit // 2)


def drag(count, table_ref, gas_ref, gvr_ref, gva_ref, vr_ref, va_ref, messages, vr_out, va_out, gvr_out, gva_out, sums_ref, halves_in_ref, halves_out_ref):
    bins, rows, _ = vr_ref.shape
    for offset in range(count):
        read_sums(messages[offset], inner_rows(rows), bins, halves_in_ref, sums_ref.at[offset])
        read_sums(messages[count + offset], outer_rows(rows), bins, halves_out_ref, sums_ref.at[offset])
    sums = [total_sums(lambda o, n=n: sums_ref[o, n], 0, count // 2) for n in range(3)]
    gas = gas_ref[...]
    denom = gas + sums[2]
    new_r = (gas * gvr_ref[...] + sums[0]) / denom
    new_a = (gas * gva_ref[...] + sums[1]) / denom
    gvr_out[...] = new_r
    gva_out[...] = new_a
    for b in range(bins):
        coupling = jnp.broadcast_to(table_ref[0, b:b + 1, :], gas.shape)
        scale = jnp.broadcast_to(table_ref[1, b:b + 1, :], gas.shape)
        vr_out[b] = vr_ref[b] * scale + coupling * new_r
        va_out[b] = va_ref[b] * scale + coupling * new_a


def weights_kernel(rows_ref, swapped_ref, out_ref):
    lines, total = rows_ref.shape
    bins = lines // total
    here = lax.axis_index("bin")
    shift_of = (bins - 1).bit_length()
    taker = lax.shift_right_logical(lax.broadcasted_iota(jnp.int32, (lines, total), 0), 2 * shift_of) ^ here
    giver = lax.shift_right_logical(lax.broadcasted_iota(jnp.int32, (lines, total), 1), shift_of) ^ here
    one = rows_ref[...].astype(F32)
    both = one + swapped_ref[...].astype(F32)
    high = both.astype(BF16).astype(F32)
    earlier = giver < taker
    zero = jnp.zeros_like(one)
    out_ref[:, :total] = jnp.where(giver == taker, one, jnp.where(earlier, high, zero)).astype(BF16)
    out_ref[:, total:] = jnp.where(earlier, both - high, zero).astype(BF16)


def block_start(offset, bins):
    return pl.multiple_of((lax.axis_index("bin") ^ offset) * bins, bins)


def add_blocks(weights_ref, messages, count, first, last, dens_ref, gain_ref, old_ref):
    n_rows, bins, cells = gain_ref.shape
    total = dens_ref.shape[1] // 2
    group = 8
    for offset in range(count):
        at = block_start(offset, bins)
        for n in range(n_rows):
            if offset < last:
                low = messages[offset][n * bins:(n + 1) * bins, :]
            else:
                low = jnp.zeros((bins, cells), BF16)
            dens_ref[n, pl.ds(at, bins), :] = low
            dens_ref[n, pl.ds(total + at, bins), :] = low
    for n in range(n_rows):
        both = dens_ref[n]
        acc = jnp.zeros((bins, cells), F32) if old_ref is None else old_ref[n]
        for offset in range(first, last):
            wide = messages[offset][n * bins:(n + 1) * bins, :].astype(F32)
            at = block_start(offset, bins) * bins
            for i in range(0, bins, group):
                lines = pl.ds(pl.multiple_of(at + i * bins, group * bins), group * bins)
                inner = jnp.dot(weights_ref[lines, :], both, preferred_element_type=F32)
                for g in range(group):
                    acc = acc + inner[g * bins:(g + 1) * bins] * wide[i + g:i + g + 1]
        gain_ref[n] = acc


def first_gain_kernel(count, weights_ref, *refs):
    messages, (gain_in_ref, gain_out_ref, dens_in_ref, dens_out_ref) = refs[:-4], refs[-4:]
    half = count // 2
    add_blocks(weights_ref, messages[half + 1:], count, 0, half, dens_out_ref, gain_out_ref, None)
    add_blocks(weights_ref, messages[:half + 1], count, 0, half + 1, dens_in_ref, gain_in_ref, None)


def second_gain_kernel(weights_ref, old_ref, *refs):
    messages, (gain_ref, dens_ref) = refs[:-2], refs[-2:]
    count = len(messages)
    add_blocks(weights_ref, messages, count, count // 2, count, dens_ref, gain_ref, old_ref)


def last_kernel(
    count, table_ref, gas_ref, gvr_ref, gva_ref, vr_ref, va_ref, weights_ref, adv_in_ref, adv_out_ref, gain_in_ref, gain_out_ref, *refs
):
    messages, refs = refs[:-16], refs[-16:]
    outs, kept, refs = refs[:5], refs[5:10], refs[10:]
    new_in_ref, dens_in_ref, sums_ref, halves_in_ref, halves_out_ref, sems = refs
    rows = vr_ref.shape[1]
    copies = [pltpu.make_async_copy(kept[n], outs[n], sems.at[n]) for n in range(5)]
    density_ref, vr_out, va_out, gvr_out, gva_out = kept
    drag(
        count, table_ref, gas_ref, gvr_ref, gva_ref, vr_ref, va_ref, messages,
        vr_out, va_out, gvr_out, gva_out, sums_ref, halves_in_ref, halves_out_ref,
    )
    for copy in copies[1:]:
        copy.start()
    add_blocks(weights_ref, messages[:count], count, count // 2 + 1, count, dens_in_ref, new_in_ref, gain_in_ref)
    for n, r in enumerate(inner_rows(rows)):
        density_ref[:, r, :] = adv_in_ref[n] + COAGULATION * new_in_ref[n]
    for n, r in enumerate(outer_rows(rows)):
        density_ref[:, r, :] = adv_out_ref[n] + COAGULATION * gain_out_ref[n]
    copies[0].start()
    for copy in copies:
        copy.wait()


def struct(shape, dtype=F32):
    return jax.ShapeDtypeStruct(shape, dtype)


def call(kernel, outs, *args, scratch=(), remote=(), loose=(), spec=VMEM):
    specs = [ANY if n in remote else VMEM for n in range(len(args))]
    placed = [x if n in remote or n in loose else pltpu.with_memory_space_constraint(x, pltpu.VMEM) for n, x in enumerate(args)]
    return pl.pallas_call(
        kernel,
        out_shape=outs,
        in_specs=specs,
        out_specs=jax.tree.map(lambda _: spec, outs, is_leaf=lambda x: hasattr(x, "dtype")),
        scratch_shapes=scratch,
    )(*placed)


def xor_pairs(axis, bit):
    return [(i, i ^ bit) for i in range(lax.axis_size(axis))]


def even_pairs(axis):
    return xor_pairs(axis, 1)


def odd_pairs(axis):
    count = lax.axis_size(axis)
    pairs = [(0, count - 1), (count - 1, 0)]
    for i in range(1, count - 1, 2):
        pairs += [(i, i + 1), (i + 1, i)]
    return pairs


def body(rho, vr, va, gas, gvr, gva, stop_time, coef):
    bins, rows, cells = rho.shape
    total = coef.shape[1]
    inner, outer = inner_rows(rows), outer_rows(rows)
    weights_size = (total * bins, 2 * total)
    small = 2 * weights_size[0] * weights_size[1] <= SMALL_BYTES
    weights = call(
        weights_kernel, (pltpu.VMEM if small else struct)(weights_size, BF16),
        jnp.transpose(coef, (1, 0, 2)).reshape(total * bins, total), jnp.transpose(coef, (2, 0, 1)).reshape(total * bins, total),
    )
    field, kept = struct(rho.shape), pltpu.VMEM(rho.shape, F32)
    flat = struct(gas.shape)
    halo = pltpu.VMEM((3, bins, cells), BF16)
    inner_lines, outer_lines = lines_of(bins, inner), lines_of(bins, outer)
    halves_in, halves_out = (pltpu.VMEM((6 * len(picked), cells), F32) for picked in (inner, outer))

    edges = [pltpu.VMEM((2 * width, bins, cells), F32) for width in (HALO + 1, HALO, HALO)]
    to_a, to_b, rho_edge, vr_edge, va_edge, table = call(
        load_kernel, (halo, halo, *edges, pltpu.VMEM((2, bins, cells), F32)), rho, vr, va, stop_time[None],
        scratch=[pltpu.VMEM((1, bins), F32), pltpu.SemaphoreType.DMA, pltpu.SemaphoreType.DMA((6 * HALO + 2,))],
        remote=(0, 1, 2, 3),
    )
    from_b = lax.ppermute(to_b, "tile", odd_pairs("tile"))
    from_a = lax.ppermute(to_a, "tile", even_pairs("tile"))

    groups = lax.axis_size("bin")
    half = groups // 2
    dense = [pltpu.VMEM((len(picked), bins, cells), F32) for picked in (inner, outer)]
    low_in, adv_in, part_out = call(
        inner_kernel, (pltpu.VMEM((inner_lines, cells), BF16), *dense), table, rho, vr, va,
        scratch=[kept, halves_in],
    )
    near_in = [lax.ppermute(low_in, "bin", xor_pairs("bin", at)) for at in range(1, half)]
    far_in = lax.ppermute(low_in, "bin", xor_pairs("bin", half))

    adv_out, low_out = call(
        outer_kernel, (dense[1], pltpu.VMEM((outer_lines, cells), BF16)),
        table, rho_edge, vr_edge, va_edge, part_out, from_a, from_b, scratch=[halves_out],
    )
    near_out = [lax.ppermute(low_out, "bin", xor_pairs("bin", at)) for at in range(1, half)]
    far_out = [lax.ppermute(low_out, "bin", xor_pairs("bin", at)) for at in range(half, groups)]
    passed_in = [lax.ppermute(far_in, "bin", xor_pairs("bin", at)) for at in range(1, half)]

    in_messages = [low_in] + near_in + [far_in] + passed_in
    out_messages = [low_out] + near_out + far_out

    dens = [pltpu.VMEM((len(picked), 2 * total, cells), BF16) for picked in (inner, outer)]
    gain_in, gain_out = call(
        functools.partial(first_gain_kernel, groups), tuple(dense), weights, *in_messages[:half + 1], *out_messages[:half],
        scratch=dens, loose=() if small else (0,),
    )
    gain_out = call(
        second_gain_kernel, dense[1], weights, gain_out, *out_messages, scratch=dens[1:], loose=() if small else (0,),
    )
    return call(
        functools.partial(last_kernel, groups), (field, field, field, flat, flat),
        table, gas, gvr, gva, vr, va, weights, adv_in, adv_out, gain_in, gain_out, *in_messages, *out_messages,
        scratch=[kept] * 3 + [pltpu.VMEM(gas.shape, F32)] * 2 + dense[:1] + dens[:1]
        + [pltpu.VMEM((groups, 3, rows, cells), F32), halves_in, halves_out, pltpu.SemaphoreType.DMA((5,))],
        loose=() if small else (6,), spec=ANY,
    )


def solution(mesh):
    field, flat = P("bin", "tile", None), P("tile", None)
    return jax.shard_map(
        body,
        mesh=mesh,
        in_specs=(field, field, field, flat, flat, flat, P("bin"), P("bin", None, None)),
        out_specs=(field, field, field, flat, flat),
        check_vma=False,
    )
```

```python
import functools

import jax
import jax.numpy as jnp
from jax import lax
from jax.experimental import pallas as pl
from jax.experimental.pallas import tpu as pltpu
from jax.sharding import PartitionSpec as P


COURANT = 0.2
COAGULATION = 0.5
HALO = 2
SMALL_BYTES = 2**19
F32 = jnp.float32
BF16 = jnp.bfloat16

VMEM = pl.BlockSpec(memory_space=pltpu.VMEM)
ANY = pl.BlockSpec(memory_space=pl.ANY)


def minmod(a, b):
    return jnp.maximum(jnp.minimum(a, b), 0.0) + jnp.minimum(jnp.maximum(a, b), 0.0)


def face_flux(low, low_slope, high, high_slope, u):
    cu = COURANT * u
    left = low + (0.5 - 0.5 * cu) * low_slope
    right = high - (0.5 + 0.5 * cu) * high_slope
    return jnp.maximum(u, 0.0) * left + jnp.minimum(u, 0.0) * right


def shift(x, by, axis):
    return pltpu.roll(x, by % x.shape[axis], axis)


def edge_rows(rows, width):
    return list(range(width)) + list(range(rows - width, rows))


def load_kernel(rho_in, vr_in, va_in, stop_in, to_a_ref, to_b_ref, rho_ref, vr_ref, va_ref, table_ref, stop_ref, stop_sem, sems):
    _, bins, cells = rho_ref.shape
    rows = rho_in.shape[1]
    stop_copy = pltpu.make_async_copy(stop_in, stop_ref, stop_sem)
    copies = []
    for source, target in ((rho_in, rho_ref), (vr_in, vr_ref), (va_in, va_ref)):
        for n, r in enumerate(edge_rows(rows, target.shape[0] // 2)):
            copies.append(pltpu.make_async_copy(source.at[:, r, :], target.at[n], sems.at[len(copies)]))
    for copy in copies:
        copy.start()
    stop_copy.start()
    stop_copy.wait()
    square = (bins, bins)
    own = lax.broadcasted_iota(jnp.int32, square, 0) == lax.broadcasted_iota(jnp.int32, square, 1)
    stop = jnp.sum(jnp.where(own, jnp.broadcast_to(stop_ref[...], square), 0.0), axis=1, keepdims=True)
    rate = 1.0 / stop
    scale = 1.0 / (1.0 + rate)
    table_ref[0] = jnp.broadcast_to(rate * scale, (bins, cells))
    table_ref[1] = jnp.broadcast_to(scale, (bins, cells))
    for copy in copies:
        copy.wait()
    even = lax.axis_index("tile") % 2 == 0
    up = (rho_ref[0], rho_ref[1], vr_ref[0])
    last, last_v = rho_ref.shape[0] - 1, vr_ref.shape[0] - 1
    down = (rho_ref[last], rho_ref[last - 1], vr_ref[last_v])
    for n in range(3):
        to_a_ref[n] = jnp.where(even, down[n], up[n]).astype(BF16)
        to_b_ref[n] = jnp.where(even, up[n], down[n]).astype(BF16)


def radial_inside(q, v):
    rows = q.shape[0]
    row = lax.broadcasted_iota(jnp.int32, q.shape, 0)
    q_next = shift(q, -1, 0)
    d = q_next - q
    s = minmod(shift(d, 1, 0), d)
    flux = face_flux(q, s, q_next, shift(s, -1, 0), 0.5 * (v + shift(v, -1, 0)))
    flux = jnp.where((row >= HALO - 1) & (row < rows - HALO), flux, 0.0)
    return flux - shift(flux, 1, 0)


def azimuthal(q, v):
    q_next = shift(q, -1, 1)
    d = q_next - q
    s = minmod(shift(d, 1, 1), d)
    flux = face_flux(q, s, q_next, shift(s, -1, 1), 0.5 * (v + shift(v, -1, 1)))
    return flux - shift(flux, 1, 1)


def inner_rows(rows):
    return list(range(HALO, rows - HALO))


def outer_rows(rows):
    return edge_rows(rows, HALO)


def lines_of(bins, picked):
    return (bins + 6) * len(picked)


def write_message(ref, densities, sums, halves_ref):
    bins, count = densities[0].shape[0], len(densities)
    for m in range(count):
        ref[m * bins:(m + 1) * bins, :] = densities[m].astype(BF16)
        for n in range(3):
            high = sums[n][m].astype(BF16).astype(F32)
            for half, value in enumerate((high, sums[n][m] - high)):
                at = (2 * n + half) * count + m
                halves_ref[at:at + 1, :] = value
    ref[count * bins:, :] = halves_ref[...].astype(BF16)


def read_sums(ref, picked, bins, halves_ref, sums_ref):
    count = len(picked)
    halves_ref[...] = ref[count * bins:, :].astype(F32)
    for n in range(3):
        for m, r in enumerate(picked):
            high, low = 2 * n * count + m, (2 * n + 1) * count + m
            sums_ref[n, r:r + 1, :] = halves_ref[high:high + 1, :] + halves_ref[low:low + 1, :]


def weighed(sums, adv, vr, va, coupling):
    weight = adv * coupling
    return (sums[0] + weight * vr, sums[1] + weight * va, sums[2] + weight)


def inner_kernel(table_ref, rho_ref, vr_ref, va_ref, message_ref, plain_ref, adv_ref, part_ref, all_ref, halves_ref):
    bins, rows, cells = rho_ref.shape
    zero = jnp.zeros((rows, cells), F32)
    sums = (zero, zero, zero)
    for b in range(bins):
        q, vr, va = rho_ref[b], vr_ref[b], va_ref[b]
        adv = q - COURANT * (azimuthal(q, va) + radial_inside(q, vr))
        all_ref[b] = adv
        sums = weighed(sums, adv, vr, va, jnp.broadcast_to(table_ref[0, b:b + 1, :], q.shape))
    picked = inner_rows(rows)
    densities = [all_ref[:, r, :] for r in picked]
    for n, density in enumerate(densities):
        adv_ref[n] = density
    write_message(message_ref, densities, [[x[r:r + 1] for r in picked] for x in sums], halves_ref)
    plain_ref[...] = message_ref[:plain_ref.shape[0], :]
    for n, r in enumerate(outer_rows(rows)):
        part_ref[n] = all_ref[:, r, :]


def outer_kernel(table_ref, rho_ref, vr_ref, va_ref, part_ref, from_a_ref, from_b_ref, adv_ref, message_ref, halves_ref):
    tile, tiles = lax.axis_index("tile"), lax.axis_size("tile")
    even = tile % 2 == 0
    has_top = jnp.where(tile > 0, 1.0, 0.0)
    has_bottom = jnp.where(tile < tiles - 1, 1.0, 0.0)
    top, bottom = [], []
    for n in range(3):
        a, b = from_a_ref[n].astype(F32), from_b_ref[n].astype(F32)
        top.append(jnp.where(even, b, a) * has_top)
        bottom.append(jnp.where(even, a, b) * has_bottom)

    def edge(nearest, nearest_part, v, sign, halo):
        q = [halo[1], halo[0]] + nearest
        d = [sign * (q[n] - q[n + 1]) for n in range(4)]
        s = [minmod(d[n], d[n + 1]) for n in range(3)]
        speed = [0.5 * (halo[2] + v[0]), 0.5 * (v[0] + v[1])]
        flux = []
        for n in range(2):
            low, high = (n, n + 1) if sign < 0 else (n + 1, n)
            flux.append(face_flux(q[low + 1], s[low], q[high + 1], s[high], speed[n]))
        outermost = nearest_part[0] - COURANT * sign * (flux[0] - flux[1])
        return outermost, nearest_part[1] - COURANT * sign * flux[1]

    row = [rho_ref[n] for n in range(rho_ref.shape[0])]
    speed = [vr_ref[n] for n in range(vr_ref.shape[0])]
    part = [part_ref[n] for n in range(part_ref.shape[0])]
    first, second = edge(row[:3], part[:2], speed[:2], -1.0, top)
    last, before = edge(row[:2:-1], part[:1:-1], speed[:1:-1], 1.0, bottom)
    densities = [first, second, before, last]
    sums = [[], [], []]
    for n, density in enumerate(densities):
        adv_ref[n] = density
        weight = density * table_ref[0]
        for kind, value in enumerate((weight * speed[n], weight * va_ref[n], weight)):
            sums[kind].append(jnp.sum(value, axis=0, keepdims=True))
    write_message(message_ref, densities, sums, halves_ref)


def pack_kernel(own_ref, far_ref, out_ref, a_ref, b_ref):
    start = out_ref.shape[0] - a_ref.shape[0]
    count = a_ref.shape[0] // 6
    out_ref[:start, :] = far_ref[:start, :]
    a_ref[...] = own_ref[start:, :].astype(F32)
    b_ref[...] = far_ref[start:, :].astype(F32)
    for n in range(3):
        high, low = pl.ds(2 * n * count, count), pl.ds((2 * n + 1) * count, count)
        both = (a_ref[high, :] + a_ref[low, :]) + (b_ref[high, :] + b_ref[low, :])
        first = both.astype(BF16).astype(F32)
        a_ref[high, :] = first
        a_ref[low, :] = both - first
    out_ref[start:, :] = a_ref[...].astype(BF16)


def total_sums(at, offset, bit):
    if bit == 0:
        return at(offset)
    return total_sums(at, offset, bit // 2) + total_sums(at, offset ^ bit, bit // 2)


def drag(count, passing_ref, table_ref, gas_ref, gvr_ref, gva_ref, vr_ref, va_ref, messages, vr_out, va_out, gvr_out, gva_out, sums_ref, halves_in_ref, halves_out_ref):
    bins, rows, _ = vr_ref.shape
    half = count // 2
    for offset in range(half):
        passed = messages[half + offset] if offset else passing_ref
        read_sums(passed, inner_rows(rows), bins, halves_in_ref, sums_ref.at[offset])
    for offset in range(count):
        read_sums(messages[count + offset], outer_rows(rows), bins, halves_out_ref, sums_ref.at[half + offset])
    inner = [total_sums(lambda o, n=n: sums_ref[o, n], 0, half // 2) for n in range(3)]
    outer = [total_sums(lambda o, n=n: sums_ref[half + o, n], 0, half) for n in range(3)]
    row = lax.broadcasted_iota(jnp.int32, gas_ref.shape, 0)
    inside = (row >= HALO) & (row < rows - HALO)
    sums = [jnp.where(inside, inner[n], outer[n]) for n in range(3)]
    gas = gas_ref[...]
    denom = gas + sums[2]
    new_r = (gas * gvr_ref[...] + sums[0]) / denom
    new_a = (gas * gva_ref[...] + sums[1]) / denom
    gvr_out[...] = new_r
    gva_out[...] = new_a
    for b in range(bins):
        coupling = jnp.broadcast_to(table_ref[0, b:b + 1, :], gas.shape)
        scale = jnp.broadcast_to(table_ref[1, b:b + 1, :], gas.shape)
        vr_out[b] = vr_ref[b] * scale + coupling * new_r
        va_out[b] = va_ref[b] * scale + coupling * new_a


def weights_kernel(rows_ref, swapped_ref, out_ref):
    lines, total = rows_ref.shape
    bins = lines // total
    here = lax.axis_index("bin")
    shift_of = (bins - 1).bit_length()
    taker = lax.shift_right_logical(lax.broadcasted_iota(jnp.int32, (lines, total), 0), 2 * shift_of) ^ here
    giver = lax.shift_right_logical(lax.broadcasted_iota(jnp.int32, (lines, total), 1), shift_of) ^ here
    one = rows_ref[...].astype(F32)
    both = one + swapped_ref[...].astype(F32)
    high = both.astype(BF16).astype(F32)
    earlier = giver < taker
    zero = jnp.zeros_like(one)
    out_ref[:, :total] = jnp.where(giver == taker, one, jnp.where(earlier, high, zero)).astype(BF16)
    out_ref[:, total:] = jnp.where(earlier, both - high, zero).astype(BF16)


def block_start(offset, bins):
    return pl.multiple_of((lax.axis_index("bin") ^ offset) * bins, bins)


def add_blocks(weights_ref, messages, count, first, last, dens_ref, gain_ref, old_ref):
    n_rows, bins, cells = gain_ref.shape
    total = dens_ref.shape[1] // 2
    group = 8
    for offset in range(count):
        at = block_start(offset, bins)
        for n in range(n_rows):
            if offset < last:
                low = messages[offset][n * bins:(n + 1) * bins, :]
            else:
                low = jnp.zeros((bins, cells), BF16)
            dens_ref[n, pl.ds(at, bins), :] = low
            dens_ref[n, pl.ds(total + at, bins), :] = low
    for n in range(n_rows):
        both = dens_ref[n]
        acc = jnp.zeros((bins, cells), F32) if old_ref is None else old_ref[n]
        for offset in range(first, last):
            wide = messages[offset][n * bins:(n + 1) * bins, :].astype(F32)
            at = block_start(offset, bins) * bins
            for i in range(0, bins, group):
                lines = pl.ds(pl.multiple_of(at + i * bins, group * bins), group * bins)
                inner = jnp.dot(weights_ref[lines, :], both, preferred_element_type=F32)
                for g in range(group):
                    acc = acc + inner[g * bins:(g + 1) * bins] * wide[i + g:i + g + 1]
        gain_ref[n] = acc


def gain_kernel(count, weights_ref, *refs):
    messages, (gain_ref, dens_ref) = refs[:-2], refs[-2:]
    add_blocks(weights_ref, messages, count, 0, len(messages), dens_ref, gain_ref, None)


def last_kernel(
    count, passing_ref, table_ref, gas_ref, gvr_ref, gva_ref, vr_ref, va_ref, weights_ref, adv_in_ref, adv_out_ref, gain_in_ref, gain_out_ref, *refs
):
    messages, refs = refs[:-18], refs[-18:]
    outs, kept, refs = refs[:5], refs[5:10], refs[10:]
    new_in_ref, new_out_ref, dens_in_ref, dens_out_ref, sums_ref, halves_in_ref, halves_out_ref, sems = refs
    rows = vr_ref.shape[1]
    copies = [pltpu.make_async_copy(kept[n], outs[n], sems.at[n]) for n in range(5)]
    density_ref, vr_out, va_out, gvr_out, gva_out = kept
    drag(
        count, passing_ref, table_ref, gas_ref, gvr_ref, gva_ref, vr_ref, va_ref, messages,
        vr_out, va_out, gvr_out, gva_out, sums_ref, halves_in_ref, halves_out_ref,
    )
    for copy in copies[1:]:
        copy.start()
    add_blocks(weights_ref, messages[:count], count, count // 2 + 1, count, dens_in_ref, new_in_ref, gain_in_ref)
    for n, r in enumerate(inner_rows(rows)):
        density_ref[:, r, :] = adv_in_ref[n] + COAGULATION * new_in_ref[n]
    add_blocks(weights_ref, messages[count:], count, count - 1, count, dens_out_ref, new_out_ref, gain_out_ref)
    for n, r in enumerate(outer_rows(rows)):
        density_ref[:, r, :] = adv_out_ref[n] + COAGULATION * new_out_ref[n]
    copies[0].start()
    for copy in copies:
        copy.wait()


def struct(shape, dtype=F32):
    return jax.ShapeDtypeStruct(shape, dtype)


def call(kernel, outs, *args, scratch=(), remote=(), loose=(), spec=VMEM):
    specs = [ANY if n in remote else VMEM for n in range(len(args))]
    placed = [x if n in remote or n in loose else pltpu.with_memory_space_constraint(x, pltpu.VMEM) for n, x in enumerate(args)]
    return pl.pallas_call(
        kernel,
        out_shape=outs,
        in_specs=specs,
        out_specs=jax.tree.map(lambda _: spec, outs, is_leaf=lambda x: hasattr(x, "dtype")),
        scratch_shapes=scratch,
    )(*placed)


def xor_pairs(axis, bit):
    return [(i, i ^ bit) for i in range(lax.axis_size(axis))]


def even_pairs(axis):
    return xor_pairs(axis, 1)


def odd_pairs(axis):
    count = lax.axis_size(axis)
    pairs = [(0, count - 1), (count - 1, 0)]
    for i in range(1, count - 1, 2):
        pairs += [(i, i + 1), (i + 1, i)]
    return pairs


def body(rho, vr, va, gas, gvr, gva, stop_time, coef):
    bins, rows, cells = rho.shape
    total = coef.shape[1]
    inner, outer = inner_rows(rows), outer_rows(rows)
    weights_size = (total * bins, 2 * total)
    small = 2 * weights_size[0] * weights_size[1] <= SMALL_BYTES
    weights = call(
        weights_kernel, (pltpu.VMEM if small else struct)(weights_size, BF16),
        jnp.transpose(coef, (1, 0, 2)).reshape(total * bins, total), jnp.transpose(coef, (2, 0, 1)).reshape(total * bins, total),
    )
    field, kept = struct(rho.shape), pltpu.VMEM(rho.shape, F32)
    flat = struct(gas.shape)
    halo = pltpu.VMEM((3, bins, cells), BF16)
    inner_lines, outer_lines = lines_of(bins, inner), lines_of(bins, outer)
    halves_in, halves_out = (pltpu.VMEM((6 * len(picked), cells), F32) for picked in (inner, outer))

    edges = [pltpu.VMEM((2 * width, bins, cells), F32) for width in (HALO + 1, HALO, HALO)]
    to_a, to_b, rho_edge, vr_edge, va_edge, table = call(
        load_kernel, (halo, halo, *edges, pltpu.VMEM((2, bins, cells), F32)), rho, vr, va, stop_time[None],
        scratch=[pltpu.VMEM((1, bins), F32), pltpu.SemaphoreType.DMA, pltpu.SemaphoreType.DMA((6 * HALO + 2,))],
        remote=(0, 1, 2, 3),
    )
    from_b = lax.ppermute(to_b, "tile", odd_pairs("tile"))
    from_a = lax.ppermute(to_a, "tile", even_pairs("tile"))

    groups = lax.axis_size("bin")
    half = groups // 2
    dense = [pltpu.VMEM((len(picked), bins, cells), F32) for picked in (inner, outer)]
    low_in, plain_in, adv_in, part_out = call(
        inner_kernel,
        (pltpu.VMEM((inner_lines, cells), BF16), pltpu.VMEM((bins * len(inner), cells), BF16), *dense), table, rho, vr, va,
        scratch=[kept, halves_in],
    )
    near_in = [lax.ppermute(plain_in, "bin", xor_pairs("bin", at)) for at in range(1, half)]
    far_in = lax.ppermute(low_in, "bin", xor_pairs("bin", half))

    adv_out, low_out = call(
        outer_kernel, (dense[1], pltpu.VMEM((outer_lines, cells), BF16)),
        table, rho_edge, vr_edge, va_edge, part_out, from_a, from_b, scratch=[halves_out],
    )
    near_out = [lax.ppermute(low_out, "bin", xor_pairs("bin", at)) for at in range(1, half)]
    far_out = [lax.ppermute(low_out, "bin", xor_pairs("bin", at)) for at in range(half, groups)]
    passing = call(pack_kernel, pltpu.VMEM((inner_lines, cells), BF16), low_in, far_in, scratch=[halves_in] * 2)
    passed_in = [lax.ppermute(passing, "bin", xor_pairs("bin", at)) for at in range(1, half)]

    in_messages = [low_in] + near_in + [far_in] + passed_in
    out_messages = [low_out] + near_out + far_out

    dens = [pltpu.VMEM((len(picked), 2 * total, cells), BF16) for picked in (inner, outer)]
    gains = []
    for n, some in ((0, in_messages[:half + 1]), (1, out_messages[:-1])):
        gains.append(call(
            functools.partial(gain_kernel, groups), dense[n], weights, *some, scratch=dens[n:n + 1], loose=() if small else (0,),
        ))
    return call(
        functools.partial(last_kernel, groups), (field, field, field, flat, flat),
        passing, table, gas, gvr, gva, vr, va, weights, adv_in, adv_out, *gains, *in_messages, *out_messages,
        scratch=[kept] * 3 + [pltpu.VMEM(gas.shape, F32)] * 2 + dense + dens
        + [pltpu.VMEM((half + groups, 3, rows, cells), F32), halves_in, halves_out, pltpu.SemaphoreType.DMA((5,))],
        loose=() if small else (7,), spec=ANY,
    )


def solution(mesh):
    field, flat = P("bin", "tile", None), P("tile", None)
    return jax.shard_map(
        body,
        mesh=mesh,
        in_specs=(field, field, field, flat, flat, flat, P("bin"), P("bin", None, None)),
        out_specs=(field, field, field, flat, flat),
        check_vma=False,
    )
```

```python
import functools

import jax
import jax.numpy as jnp
from jax import lax
from jax.experimental import pallas as pl
from jax.experimental.pallas import tpu as pltpu
from jax.sharding import PartitionSpec as P


COURANT = 0.2
COAGULATION = 0.5
HALO = 2
SMALL_BYTES = 2**19
F32 = jnp.float32
BF16 = jnp.bfloat16

VMEM = pl.BlockSpec(memory_space=pltpu.VMEM)
ANY = pl.BlockSpec(memory_space=pl.ANY)


def minmod(a, b):
    return jnp.maximum(jnp.minimum(a, b), jnp.minimum(jnp.maximum(a, b), 0.0))


def face_flux(low, low_slope, high, high_slope, low_speed, high_speed):
    cu = low_speed + high_speed
    reach = 0.5 - 0.5 * jnp.abs(cu)
    return cu * jnp.where(cu > 0, low + reach * low_slope, high - reach * high_slope)


def shift(x, by, axis):
    return pltpu.roll(x, by % x.shape[axis], axis)


def edge_rows(rows, width):
    return list(range(width)) + list(range(rows - width, rows))


def load_kernel(rho_in, vr_in, va_in, stop_in, to_a_ref, to_b_ref, rho_ref, vr_ref, va_ref, table_ref, stop_ref, stop_sem, sems):
    _, bins, cells = rho_ref.shape
    rows = rho_in.shape[1]
    stop_copy = pltpu.make_async_copy(stop_in, stop_ref, stop_sem)
    copies = []
    for source, target in ((rho_in, rho_ref), (vr_in, vr_ref), (va_in, va_ref)):
        for n, r in enumerate(edge_rows(rows, target.shape[0] // 2)):
            copies.append(pltpu.make_async_copy(source.at[:, r, :], target.at[n], sems.at[len(copies)]))
    for copy in copies:
        copy.start()
    stop_copy.start()
    stop_copy.wait()
    square = (bins, bins)
    own = lax.broadcasted_iota(jnp.int32, square, 0) == lax.broadcasted_iota(jnp.int32, square, 1)
    stop = jnp.sum(jnp.where(own, jnp.broadcast_to(stop_ref[...], square), 0.0), axis=1, keepdims=True)
    rate = 1.0 / stop
    scale = 1.0 / (1.0 + rate)
    table_ref[0] = jnp.broadcast_to(rate * scale, (bins, cells))
    table_ref[1] = jnp.broadcast_to(scale, (bins, cells))
    for copy in copies:
        copy.wait()
    even = lax.axis_index("tile") % 2 == 0
    up = (rho_ref[0], rho_ref[1], vr_ref[0])
    last, last_v = rho_ref.shape[0] - 1, vr_ref.shape[0] - 1
    down = (rho_ref[last], rho_ref[last - 1], vr_ref[last_v])
    for n in range(3):
        to_a_ref[n] = jnp.where(even, down[n], up[n]).astype(BF16)
        to_b_ref[n] = jnp.where(even, up[n], down[n]).astype(BF16)


def radial_inside(q, v):
    rows = q.shape[0]
    row = lax.broadcasted_iota(jnp.int32, q.shape, 0)
    q_next = shift(q, -1, 0)
    d = q_next - q
    s = minmod(shift(d, 1, 0), d)
    flux = face_flux(q, s, q_next, shift(s, -1, 0), v, shift(v, -1, 0))
    flux = jnp.where((row >= HALO - 1) & (row < rows - HALO), flux, 0.0)
    return flux - shift(flux, 1, 0)


def azimuthal(q, v):
    q_next = shift(q, -1, 1)
    d = q_next - q
    s = minmod(shift(d, 1, 1), d)
    flux = face_flux(q, s, q_next, shift(s, -1, 1), v, shift(v, -1, 1))
    return flux - shift(flux, 1, 1)


def inner_rows(rows):
    return list(range(HALO, rows - HALO))


def outer_rows(rows):
    return edge_rows(rows, HALO)


def lines_of(bins, picked):
    return (bins + 6) * len(picked)


def write_message(ref, densities, sums, halves_ref):
    bins, count = densities[0].shape[0], len(densities)
    for m in range(count):
        ref[m * bins:(m + 1) * bins, :] = densities[m].astype(BF16)
        for n in range(3):
            high = sums[n][m].astype(BF16).astype(F32)
            for half, value in enumerate((high, sums[n][m] - high)):
                at = (2 * n + half) * count + m
                halves_ref[at:at + 1, :] = value
    ref[count * bins:, :] = halves_ref[...].astype(BF16)


def read_sums(ref, picked, bins, halves_ref, sums_ref):
    count = len(picked)
    halves_ref[...] = ref[count * bins:, :].astype(F32)
    for n in range(3):
        for m, r in enumerate(picked):
            high, low = 2 * n * count + m, (2 * n + 1) * count + m
            sums_ref[n, r:r + 1, :] = halves_ref[high:high + 1, :] + halves_ref[low:low + 1, :]


def weighed(sums, adv, vr, va, coupling):
    weight = adv * coupling
    return (sums[0] + weight * vr, sums[1] + weight * va, sums[2] + weight)


def inner_kernel(table_ref, rho_ref, vr_ref, va_ref, message_ref, plain_ref, adv_ref, part_ref, all_ref, halves_ref):
    bins, rows, cells = rho_ref.shape
    zero = jnp.zeros((rows, cells), F32)
    sums = (zero, zero, zero)
    for b in range(bins):
        q, vr, va = rho_ref[b], vr_ref[b], va_ref[b]
        adv = q - (azimuthal(q, 0.5 * COURANT * va) + radial_inside(q, 0.5 * COURANT * vr))
        all_ref[b] = adv
        sums = weighed(sums, adv, vr, va, jnp.broadcast_to(table_ref[0, b:b + 1, :], q.shape))
    picked = inner_rows(rows)
    densities = [all_ref[:, r, :] for r in picked]
    for n, density in enumerate(densities):
        adv_ref[n] = density
    write_message(message_ref, densities, [[x[r:r + 1] for r in picked] for x in sums], halves_ref)
    plain_ref[...] = message_ref[:plain_ref.shape[0], :]
    for n, r in enumerate(outer_rows(rows)):
        part_ref[n] = all_ref[:, r, :]


def outer_kernel(table_ref, rho_ref, vr_ref, va_ref, part_ref, from_a_ref, from_b_ref, adv_ref, message_ref, halves_ref):
    tile, tiles = lax.axis_index("tile"), lax.axis_size("tile")
    even = tile % 2 == 0
    has_top = jnp.where(tile > 0, 1.0, 0.0)
    has_bottom = jnp.where(tile < tiles - 1, 1.0, 0.0)
    top, bottom = [], []
    for n in range(3):
        a, b = from_a_ref[n].astype(F32), from_b_ref[n].astype(F32)
        top.append(jnp.where(even, b, a) * has_top)
        bottom.append(jnp.where(even, a, b) * has_bottom)

    def edge(nearest, nearest_part, v, sign, halo):
        q = [halo[1], halo[0]] + nearest
        d = [sign * (q[n] - q[n + 1]) for n in range(4)]
        s = [minmod(d[n], d[n + 1]) for n in range(3)]
        speed = [0.5 * COURANT * x for x in (halo[2], v[0], v[1])]
        flux = []
        for n in range(2):
            low, high = (n, n + 1) if sign < 0 else (n + 1, n)
            flux.append(face_flux(q[low + 1], s[low], q[high + 1], s[high], speed[n], speed[n + 1]))
        outermost = nearest_part[0] - sign * (flux[0] - flux[1])
        return outermost, nearest_part[1] - sign * flux[1]

    row = [rho_ref[n] for n in range(rho_ref.shape[0])]
    speed = [vr_ref[n] for n in range(vr_ref.shape[0])]
    part = [part_ref[n] for n in range(part_ref.shape[0])]
    first, second = edge(row[:3], part[:2], speed[:2], -1.0, top)
    last, before = edge(row[:2:-1], part[:1:-1], speed[:1:-1], 1.0, bottom)
    densities = [first, second, before, last]
    sums = [[], [], []]
    for n, density in enumerate(densities):
        adv_ref[n] = density
        weight = density * table_ref[0]
        for kind, value in enumerate((weight * speed[n], weight * va_ref[n], weight)):
            sums[kind].append(jnp.sum(value, axis=0, keepdims=True))
    write_message(message_ref, densities, sums, halves_ref)


def pack_kernel(own_ref, far_ref, out_ref, a_ref, b_ref):
    start = out_ref.shape[0] - a_ref.shape[0]
    count = a_ref.shape[0] // 6
    out_ref[:start, :] = far_ref[:start, :]
    a_ref[...] = own_ref[start:, :].astype(F32)
    b_ref[...] = far_ref[start:, :].astype(F32)
    for n in range(3):
        high, low = pl.ds(2 * n * count, count), pl.ds((2 * n + 1) * count, count)
        both = (a_ref[high, :] + a_ref[low, :]) + (b_ref[high, :] + b_ref[low, :])
        first = both.astype(BF16).astype(F32)
        a_ref[high, :] = first
        a_ref[low, :] = both - first
    out_ref[start:, :] = a_ref[...].astype(BF16)


def total_sums(at, offset, bit):
    if bit == 0:
        return at(offset)
    return total_sums(at, offset, bit // 2) + total_sums(at, offset ^ bit, bit // 2)


def drag(count, passing_ref, table_ref, gas_ref, gvr_ref, gva_ref, vr_ref, va_ref, messages, vr_out, va_out, gvr_out, gva_out, sums_ref, halves_in_ref, halves_out_ref):
    bins, rows, _ = vr_ref.shape
    half = count // 2
    for offset in range(half):
        passed = messages[half + offset] if offset else passing_ref
        read_sums(passed, inner_rows(rows), bins, halves_in_ref, sums_ref.at[offset])
    for offset in range(count):
        read_sums(messages[count + offset], outer_rows(rows), bins, halves_out_ref, sums_ref.at[half + offset])
    inner = [total_sums(lambda o, n=n: sums_ref[o, n], 0, half // 2) for n in range(3)]
    outer = [total_sums(lambda o, n=n: sums_ref[half + o, n], 0, half) for n in range(3)]
    row = lax.broadcasted_iota(jnp.int32, gas_ref.shape, 0)
    inside = (row >= HALO) & (row < rows - HALO)
    sums = [jnp.where(inside, inner[n], outer[n]) for n in range(3)]
    gas = gas_ref[...]
    denom = gas + sums[2]
    new_r = (gas * gvr_ref[...] + sums[0]) / denom
    new_a = (gas * gva_ref[...] + sums[1]) / denom
    gvr_out[...] = new_r
    gva_out[...] = new_a
    for b in range(bins):
        coupling = jnp.broadcast_to(table_ref[0, b:b + 1, :], gas.shape)
        scale = jnp.broadcast_to(table_ref[1, b:b + 1, :], gas.shape)
        vr_out[b] = vr_ref[b] * scale + coupling * new_r
        va_out[b] = va_ref[b] * scale + coupling * new_a


def weights_kernel(rows_ref, swapped_ref, out_ref):
    lines, total = rows_ref.shape
    bins = lines // total
    here = lax.axis_index("bin")
    shift_of = (bins - 1).bit_length()
    taker = lax.shift_right_logical(lax.broadcasted_iota(jnp.int32, (lines, total), 0), 2 * shift_of) ^ here
    giver = lax.shift_right_logical(lax.broadcasted_iota(jnp.int32, (lines, total), 1), shift_of) ^ here
    one = rows_ref[...].astype(F32)
    both = one + swapped_ref[...].astype(F32)
    high = both.astype(BF16).astype(F32)
    earlier = giver < taker
    zero = jnp.zeros_like(one)
    out_ref[:, :total] = jnp.where(giver == taker, one, jnp.where(earlier, high, zero)).astype(BF16)
    out_ref[:, total:] = jnp.where(earlier, both - high, zero).astype(BF16)


def block_start(offset, bins):
    return pl.multiple_of((lax.axis_index("bin") ^ offset) * bins, bins)


def add_blocks(weights_ref, messages, count, first, last, dens_ref, gain_ref, old_ref):
    n_rows, bins, cells = gain_ref.shape
    total = dens_ref.shape[1] // 2
    group = 8
    for offset in range(count):
        at = block_start(offset, bins)
        for n in range(n_rows):
            if offset < last:
                low = messages[offset][n * bins:(n + 1) * bins, :]
            else:
                low = jnp.zeros((bins, cells), BF16)
            dens_ref[n, pl.ds(at, bins), :] = low
            dens_ref[n, pl.ds(total + at, bins), :] = low
    for n in range(n_rows):
        both = dens_ref[n]
        acc = jnp.zeros((bins, cells), F32) if old_ref is None else old_ref[n]
        for offset in range(first, last):
            wide = messages[offset][n * bins:(n + 1) * bins, :].astype(F32)
            at = block_start(offset, bins) * bins
            for i in range(0, bins, group):
                lines = pl.ds(pl.multiple_of(at + i * bins, group * bins), group * bins)
                inner = jnp.dot(weights_ref[lines, :], both, preferred_element_type=F32)
                for g in range(group):
                    acc = acc + inner[g * bins:(g + 1) * bins] * wide[i + g:i + g + 1]
        gain_ref[n] = acc


def gain_kernel(count, weights_ref, *refs):
    messages, (gain_ref, dens_ref) = refs[:-2], refs[-2:]
    add_blocks(weights_ref, messages, count, 0, len(messages), dens_ref, gain_ref, None)


def last_block_kernel(weights_ref, old_ref, *refs):
    messages, (gain_ref, dens_ref) = refs[:-2], refs[-2:]
    count = len(messages)
    add_blocks(weights_ref, messages, count, count - 1, count, dens_ref, gain_ref, old_ref)


def last_kernel(
    count, passing_ref, table_ref, gas_ref, gvr_ref, gva_ref, vr_ref, va_ref, weights_ref, adv_in_ref, adv_out_ref, gain_in_ref, gain_out_ref, *refs
):
    messages, refs = refs[:-16], refs[-16:]
    outs, kept, refs = refs[:5], refs[5:10], refs[10:]
    new_in_ref, dens_in_ref, sums_ref, halves_in_ref, halves_out_ref, sems = refs
    rows = vr_ref.shape[1]
    copies = [pltpu.make_async_copy(kept[n], outs[n], sems.at[n]) for n in range(5)]
    density_ref, vr_out, va_out, gvr_out, gva_out = kept
    drag(
        count, passing_ref, table_ref, gas_ref, gvr_ref, gva_ref, vr_ref, va_ref, messages,
        vr_out, va_out, gvr_out, gva_out, sums_ref, halves_in_ref, halves_out_ref,
    )
    for copy in copies[1:]:
        copy.start()
    add_blocks(weights_ref, messages[:count], count, count // 2 + 1, count, dens_in_ref, new_in_ref, gain_in_ref)
    for n, r in enumerate(inner_rows(rows)):
        density_ref[:, r, :] = adv_in_ref[n] + COAGULATION * new_in_ref[n]
    for n, r in enumerate(outer_rows(rows)):
        density_ref[:, r, :] = adv_out_ref[n] + COAGULATION * gain_out_ref[n]
    copies[0].start()
    for copy in copies:
        copy.wait()


def struct(shape, dtype=F32):
    return jax.ShapeDtypeStruct(shape, dtype)


def call(kernel, outs, *args, scratch=(), remote=(), loose=(), spec=VMEM):
    specs = [ANY if n in remote else VMEM for n in range(len(args))]
    placed = [x if n in remote or n in loose else pltpu.with_memory_space_constraint(x, pltpu.VMEM) for n, x in enumerate(args)]
    return pl.pallas_call(
        kernel,
        out_shape=outs,
        in_specs=specs,
        out_specs=jax.tree.map(lambda _: spec, outs, is_leaf=lambda x: hasattr(x, "dtype")),
        scratch_shapes=scratch,
    )(*placed)


def xor_pairs(axis, bit):
    return [(i, i ^ bit) for i in range(lax.axis_size(axis))]


def even_pairs(axis):
    return xor_pairs(axis, 1)


def odd_pairs(axis):
    count = lax.axis_size(axis)
    pairs = [(0, count - 1), (count - 1, 0)]
    for i in range(1, count - 1, 2):
        pairs += [(i, i + 1), (i + 1, i)]
    return pairs


def body(rho, vr, va, gas, gvr, gva, stop_time, coef):
    bins, rows, cells = rho.shape
    total = coef.shape[1]
    inner, outer = inner_rows(rows), outer_rows(rows)
    weights_size = (total * bins, 2 * total)
    small = 2 * weights_size[0] * weights_size[1] <= SMALL_BYTES
    weights = call(
        weights_kernel, (pltpu.VMEM if small else struct)(weights_size, BF16),
        jnp.transpose(coef, (1, 0, 2)).reshape(total * bins, total), jnp.transpose(coef, (2, 0, 1)).reshape(total * bins, total),
    )
    field, kept = struct(rho.shape), pltpu.VMEM(rho.shape, F32)
    flat = struct(gas.shape)
    halo = pltpu.VMEM((3, bins, cells), BF16)
    inner_lines, outer_lines = lines_of(bins, inner), lines_of(bins, outer)
    halves_in, halves_out = (pltpu.VMEM((6 * len(picked), cells), F32) for picked in (inner, outer))

    edges = [pltpu.VMEM((2 * width, bins, cells), F32) for width in (HALO + 1, HALO, HALO)]
    to_a, to_b, rho_edge, vr_edge, va_edge, table = call(
        load_kernel, (halo, halo, *edges, pltpu.VMEM((2, bins, cells), F32)), rho, vr, va, stop_time[None],
        scratch=[pltpu.VMEM((1, bins), F32), pltpu.SemaphoreType.DMA, pltpu.SemaphoreType.DMA((6 * HALO + 2,))],
        remote=(0, 1, 2, 3),
    )
    from_b = lax.ppermute(to_b, "tile", odd_pairs("tile"))
    from_a = lax.ppermute(to_a, "tile", even_pairs("tile"))

    groups = lax.axis_size("bin")
    half = groups // 2
    dense = [pltpu.VMEM((len(picked), bins, cells), F32) for picked in (inner, outer)]
    low_in, plain_in, adv_in, part_out = call(
        inner_kernel,
        (pltpu.VMEM((inner_lines, cells), BF16), pltpu.VMEM((bins * len(inner), cells), BF16), *dense), table, rho, vr, va,
        scratch=[kept, halves_in],
    )
    near_in = [lax.ppermute(plain_in, "bin", xor_pairs("bin", at)) for at in range(1, half)]
    far_in = lax.ppermute(low_in, "bin", xor_pairs("bin", half))

    adv_out, low_out = call(
        outer_kernel, (dense[1], pltpu.VMEM((outer_lines, cells), BF16)),
        table, rho_edge, vr_edge, va_edge, part_out, from_a, from_b, scratch=[halves_out],
    )
    near_out = [lax.ppermute(low_out, "bin", xor_pairs("bin", at)) for at in range(1, half)]
    far_out = [lax.ppermute(low_out, "bin", xor_pairs("bin", at)) for at in range(half, groups)]
    passing = call(pack_kernel, pltpu.VMEM((inner_lines, cells), BF16), low_in, far_in, scratch=[halves_in] * 2)
    passed_in = [lax.ppermute(passing, "bin", xor_pairs("bin", at)) for at in range(1, half)]

    in_messages = [low_in] + near_in + [far_in] + passed_in
    out_messages = [low_out] + near_out + far_out

    dens = [pltpu.VMEM((len(picked), 2 * total, cells), BF16) for picked in (inner, outer)]
    gains = []
    for n, some in ((0, in_messages[:half + 1]), (1, out_messages[:-1])):
        gains.append(call(
            functools.partial(gain_kernel, groups), dense[n], weights, *some, scratch=dens[n:n + 1], loose=() if small else (0,),
        ))
    gains[1] = call(
        last_block_kernel, dense[1], weights, gains[1], *out_messages, scratch=dens[1:], loose=() if small else (0,),
    )
    return call(
        functools.partial(last_kernel, groups), (field, field, field, flat, flat),
        passing, table, gas, gvr, gva, vr, va, weights, adv_in, adv_out, *gains, *in_messages, *out_messages,
        scratch=[kept] * 3 + [pltpu.VMEM(gas.shape, F32)] * 2 + dense[:1] + dens[:1]
        + [pltpu.VMEM((half + groups, 3, rows, cells), F32), halves_in, halves_out, pltpu.SemaphoreType.DMA((5,))],
        loose=() if small else (7,), spec=ANY,
    )


def solution(mesh):
    field, flat = P("bin", "tile", None), P("tile", None)
    return jax.shard_map(
        body,
        mesh=mesh,
        in_specs=(field, field, field, flat, flat, flat, P("bin"), P("bin", None, None)),
        out_specs=(field, field, field, flat, flat),
        check_vma=False,
    )
```

```python
import functools

import jax
import jax.numpy as jnp
from jax import lax
from jax.experimental import pallas as pl
from jax.experimental.pallas import tpu as pltpu
from jax.sharding import PartitionSpec as P


COURANT = 0.2
COAGULATION = 0.5
HALO = 2
SMALL_BYTES = 2**19
F32 = jnp.float32
BF16 = jnp.bfloat16

VMEM = pl.BlockSpec(memory_space=pltpu.VMEM)
ANY = pl.BlockSpec(memory_space=pl.ANY)


def minmod(a, b):
    return jnp.maximum(jnp.minimum(a, b), jnp.minimum(jnp.maximum(a, b), 0.0))


def face_flux(low, low_slope, high, high_slope, low_speed, high_speed):
    cu = low_speed + high_speed
    reach = 0.5 - 0.5 * jnp.abs(cu)
    return cu * jnp.where(cu > 0, low + reach * low_slope, high - reach * high_slope)


def shift(x, by, axis):
    return pltpu.roll(x, by % x.shape[axis], axis)


def edge_rows(rows, width):
    return list(range(width)) + list(range(rows - width, rows))


def load_kernel(rho_in, vr_in, va_in, stop_in, to_a_ref, to_b_ref, rho_ref, vr_ref, va_ref, table_ref, stop_ref, stop_sem, sems):
    _, bins, cells = rho_ref.shape
    rows = rho_in.shape[1]
    stop_copy = pltpu.make_async_copy(stop_in, stop_ref, stop_sem)
    copies = []
    for source, target in ((rho_in, rho_ref), (vr_in, vr_ref), (va_in, va_ref)):
        for n, r in enumerate(edge_rows(rows, target.shape[0] // 2)):
            copies.append(pltpu.make_async_copy(source.at[:, r, :], target.at[n], sems.at[len(copies)]))
    for copy in copies:
        copy.start()
    stop_copy.start()
    stop_copy.wait()
    square = (bins, bins)
    own = lax.broadcasted_iota(jnp.int32, square, 0) == lax.broadcasted_iota(jnp.int32, square, 1)
    stop = jnp.sum(jnp.where(own, jnp.broadcast_to(stop_ref[...], square), 0.0), axis=1, keepdims=True)
    rate = 1.0 / stop
    scale = 1.0 / (1.0 + rate)
    table_ref[0] = jnp.broadcast_to(rate * scale, (bins, cells))
    table_ref[1] = jnp.broadcast_to(scale, (bins, cells))
    for copy in copies:
        copy.wait()
    even = lax.axis_index("tile") % 2 == 0
    up = (rho_ref[0], rho_ref[1], vr_ref[0])
    last, last_v = rho_ref.shape[0] - 1, vr_ref.shape[0] - 1
    down = (rho_ref[last], rho_ref[last - 1], vr_ref[last_v])
    for n in range(3):
        to_a_ref[n] = jnp.where(even, down[n], up[n]).astype(BF16)
        to_b_ref[n] = jnp.where(even, up[n], down[n]).astype(BF16)


def radial_inside(q, v):
    rows = q.shape[0]
    row = lax.broadcasted_iota(jnp.int32, q.shape, 0)
    q_next = shift(q, -1, 0)
    d = q_next - q
    s = minmod(shift(d, 1, 0), d)
    flux = face_flux(q, s, q_next, shift(s, -1, 0), v, shift(v, -1, 0))
    flux = jnp.where((row >= HALO - 1) & (row < rows - HALO), flux, 0.0)
    return flux - shift(flux, 1, 0)


def azimuthal(q, v):
    q_next = shift(q, -1, 1)
    d = q_next - q
    s = minmod(shift(d, 1, 1), d)
    flux = face_flux(q, s, q_next, shift(s, -1, 1), v, shift(v, -1, 1))
    return flux - shift(flux, 1, 1)


def inner_rows(rows):
    return list(range(HALO, rows - HALO))


def outer_rows(rows):
    return edge_rows(rows, HALO)


def lines_of(bins, picked):
    return (bins + 6) * len(picked)


def write_message(ref, densities, sums, halves_ref):
    bins, count = densities[0].shape[0], len(densities)
    for m in range(count):
        ref[m * bins:(m + 1) * bins, :] = densities[m].astype(BF16)
        for n in range(3):
            high = sums[n][m].astype(BF16).astype(F32)
            for half, value in enumerate((high, sums[n][m] - high)):
                at = (2 * n + half) * count + m
                halves_ref[at:at + 1, :] = value
    ref[count * bins:, :] = halves_ref[...].astype(BF16)


def read_sums(ref, picked, bins, halves_ref, sums_ref):
    count = len(picked)
    halves_ref[...] = ref[count * bins:, :].astype(F32)
    for n in range(3):
        for m, r in enumerate(picked):
            high, low = 2 * n * count + m, (2 * n + 1) * count + m
            sums_ref[n, r:r + 1, :] = halves_ref[high:high + 1, :] + halves_ref[low:low + 1, :]


def weighed(sums, adv, vr, va, coupling):
    weight = adv * coupling
    return (sums[0] + weight * vr, sums[1] + weight * va, sums[2] + weight)


def inner_kernel(table_ref, rho_ref, vr_ref, va_ref, message_ref, plain_ref, adv_ref, part_ref, all_ref, halves_ref):
    bins, rows, cells = rho_ref.shape
    zero = jnp.zeros((rows, cells), F32)
    sums = (zero, zero, zero)
    for b in range(bins):
        q, vr, va = rho_ref[b], vr_ref[b], va_ref[b]
        adv = q - (azimuthal(q, 0.5 * COURANT * va) + radial_inside(q, 0.5 * COURANT * vr))
        all_ref[b] = adv
        sums = weighed(sums, adv, vr, va, jnp.broadcast_to(table_ref[0, b:b + 1, :], q.shape))
    picked = inner_rows(rows)
    densities = [all_ref[:, r, :] for r in picked]
    for n, density in enumerate(densities):
        adv_ref[n] = density
    write_message(message_ref, densities, [[x[r:r + 1] for r in picked] for x in sums], halves_ref)
    plain_ref[...] = message_ref[:plain_ref.shape[0], :]
    for n, r in enumerate(outer_rows(rows)):
        part_ref[n] = all_ref[:, r, :]


def outer_kernel(table_ref, rho_ref, vr_ref, va_ref, part_ref, from_a_ref, from_b_ref, adv_ref, message_ref, halves_ref):
    tile, tiles = lax.axis_index("tile"), lax.axis_size("tile")
    even = tile % 2 == 0
    has_top = jnp.where(tile > 0, 1.0, 0.0)
    has_bottom = jnp.where(tile < tiles - 1, 1.0, 0.0)
    top, bottom = [], []
    for n in range(3):
        a, b = from_a_ref[n].astype(F32), from_b_ref[n].astype(F32)
        top.append(jnp.where(even, b, a) * has_top)
        bottom.append(jnp.where(even, a, b) * has_bottom)

    def edge(nearest, nearest_part, v, sign, halo):
        q = [halo[1], halo[0]] + nearest
        d = [sign * (q[n] - q[n + 1]) for n in range(4)]
        s = [minmod(d[n], d[n + 1]) for n in range(3)]
        speed = [0.5 * COURANT * x for x in (halo[2], v[0], v[1])]
        flux = []
        for n in range(2):
            low, high = (n, n + 1) if sign < 0 else (n + 1, n)
            flux.append(face_flux(q[low + 1], s[low], q[high + 1], s[high], speed[n], speed[n + 1]))
        outermost = nearest_part[0] - sign * (flux[0] - flux[1])
        return outermost, nearest_part[1] - sign * flux[1]

    row = [rho_ref[n] for n in range(rho_ref.shape[0])]
    speed = [vr_ref[n] for n in range(vr_ref.shape[0])]
    part = [part_ref[n] for n in range(part_ref.shape[0])]
    first, second = edge(row[:3], part[:2], speed[:2], -1.0, top)
    last, before = edge(row[:2:-1], part[:1:-1], speed[:1:-1], 1.0, bottom)
    densities = [first, second, before, last]
    sums = [[], [], []]
    for n, density in enumerate(densities):
        adv_ref[n] = density
        weight = density * table_ref[0]
        for kind, value in enumerate((weight * speed[n], weight * va_ref[n], weight)):
            sums[kind].append(jnp.sum(value, axis=0, keepdims=True))
    write_message(message_ref, densities, sums, halves_ref)


def pack_kernel(own_ref, far_ref, out_ref, a_ref, b_ref):
    start = out_ref.shape[0] - a_ref.shape[0]
    count = a_ref.shape[0] // 6
    out_ref[:start, :] = far_ref[:start, :]
    a_ref[...] = own_ref[start:, :].astype(F32)
    b_ref[...] = far_ref[start:, :].astype(F32)
    for n in range(3):
        high, low = pl.ds(2 * n * count, count), pl.ds((2 * n + 1) * count, count)
        both = (a_ref[high, :] + a_ref[low, :]) + (b_ref[high, :] + b_ref[low, :])
        first = both.astype(BF16).astype(F32)
        a_ref[high, :] = first
        a_ref[low, :] = both - first
    out_ref[start:, :] = a_ref[...].astype(BF16)


def total_sums(at, offset, bit):
    if bit == 0:
        return at(offset)
    return total_sums(at, offset, bit // 2) + total_sums(at, offset ^ bit, bit // 2)


def new_gas(passed, total_ref, gases_ref, bins, sums_ref, halves_ref):
    gas = gases_ref[0]
    rows = gas.shape[0]
    for offset, message in enumerate(passed):
        read_sums(message, inner_rows(rows), bins, halves_ref, sums_ref.at[offset])
    row = lax.broadcasted_iota(jnp.int32, gas.shape, 0)
    inside = (row >= HALO) & (row < rows - HALO)
    sums = []
    for n in range(3):
        inner = total_sums(lambda o, n=n: sums_ref[o, n], 0, len(passed) // 2)
        sums.append(jnp.where(inside, inner, total_ref[n]))
    denom = gas + sums[2]
    return (gas * gases_ref[1] + sums[0]) / denom, (gas * gases_ref[2] + sums[1]) / denom


def weights_kernel(rows_ref, swapped_ref, gas_ref, gvr_ref, gva_ref, out_ref, gases_ref):
    for n, ref in enumerate((gas_ref, gvr_ref, gva_ref)):
        gases_ref[n] = ref[...]
    lines, total = rows_ref.shape
    bins = lines // total
    here = lax.axis_index("bin")
    shift_of = (bins - 1).bit_length()
    taker = lax.shift_right_logical(lax.broadcasted_iota(jnp.int32, (lines, total), 0), 2 * shift_of) ^ here
    giver = lax.shift_right_logical(lax.broadcasted_iota(jnp.int32, (lines, total), 1), shift_of) ^ here
    one = rows_ref[...].astype(F32)
    both = one + swapped_ref[...].astype(F32)
    high = both.astype(BF16).astype(F32)
    earlier = giver < taker
    zero = jnp.zeros_like(one)
    out_ref[:, :total] = jnp.where(giver == taker, one, jnp.where(earlier, high, zero)).astype(BF16)
    out_ref[:, total:] = jnp.where(earlier, both - high, zero).astype(BF16)


def block_start(offset, bins):
    return pl.multiple_of((lax.axis_index("bin") ^ offset) * bins, bins)


def add_blocks(weights_ref, messages, count, first, last, dens_ref, gain_ref, old_ref):
    n_rows, bins, cells = gain_ref.shape
    total = dens_ref.shape[1] // 2
    group = 8
    for offset in range(count):
        at = block_start(offset, bins)
        for n in range(n_rows):
            if offset < last:
                low = messages[offset][n * bins:(n + 1) * bins, :]
            else:
                low = jnp.zeros((bins, cells), BF16)
            dens_ref[n, pl.ds(at, bins), :] = low
            dens_ref[n, pl.ds(total + at, bins), :] = low
    for n in range(n_rows):
        both = dens_ref[n]
        acc = jnp.zeros((bins, cells), F32) if old_ref is None else old_ref[n]
        for offset in range(first, last):
            wide = messages[offset][n * bins:(n + 1) * bins, :].astype(F32)
            at = block_start(offset, bins) * bins
            for i in range(0, bins, group):
                lines = pl.ds(pl.multiple_of(at + i * bins, group * bins), group * bins)
                inner = jnp.dot(weights_ref[lines, :], both, preferred_element_type=F32)
                for g in range(group):
                    acc = acc + inner[g * bins:(g + 1) * bins] * wide[i + g:i + g + 1]
        gain_ref[n] = acc


def gain_kernel(count, weights_ref, *refs):
    messages, (gain_ref, dens_ref) = refs[:-2], refs[-2:]
    add_blocks(weights_ref, messages, count, 0, len(messages), dens_ref, gain_ref, None)


def last_block_kernel(weights_ref, old_ref, *refs):
    messages, (gain_ref, total_ref, dens_ref, sums_ref, halves_ref) = refs[:-5], refs[-5:]
    count, bins = len(messages), gain_ref.shape[1]
    add_blocks(weights_ref, messages, count, count - 1, count, dens_ref, gain_ref, old_ref)
    for offset in range(count):
        read_sums(messages[offset], outer_rows(total_ref.shape[1]), bins, halves_ref, sums_ref.at[offset])
    for n in range(3):
        total_ref[n] = total_sums(lambda o, n=n: sums_ref[o, n], 0, count // 2)


def last_kernel(
    count, pieces, passing_ref, total_ref, table_ref, gases_ref, vr_ref, va_ref, weights_ref, adv_in_ref, adv_out_ref,
    gain_in_ref, gain_out_ref, *refs
):
    messages, refs = refs[:count], refs[count:]
    outs, kept, (new_in_ref, dens_ref, sums_ref, halves_ref, sems) = refs[:5], refs[5:10], refs[10:]
    density_ref, vr_out, va_out, gvr_out, gva_out = kept
    bins, rows, _ = vr_ref.shape
    copies = []

    def send_out(n, part=None):
        source, target = (kept[n], outs[n]) if part is None else (kept[n].at[part], outs[n].at[part])
        copies.append(pltpu.make_async_copy(source, target, sems.at[len(copies)]))
        copies[-1].start()

    add_blocks(weights_ref, messages, count, count // 2 + 1, count, dens_ref, new_in_ref, gain_in_ref)
    for n, r in enumerate(inner_rows(rows)):
        density_ref[:, r, :] = adv_in_ref[n] + COAGULATION * new_in_ref[n]
    for n, r in enumerate(outer_rows(rows)):
        density_ref[:, r, :] = adv_out_ref[n] + COAGULATION * gain_out_ref[n]
    send_out(0)
    passed = (passing_ref, *messages[count // 2 + 1:])
    new_r, new_a = new_gas(passed, total_ref, gases_ref, bins, sums_ref, halves_ref)
    gvr_out[...] = new_r
    gva_out[...] = new_a
    send_out(3)
    send_out(4)
    part = bins // pieces
    for start in range(0, bins, part):
        for b in range(start, start + part):
            coupling = jnp.broadcast_to(table_ref[0, b:b + 1, :], new_r.shape)
            scale = jnp.broadcast_to(table_ref[1, b:b + 1, :], new_r.shape)
            vr_out[b] = vr_ref[b] * scale + coupling * new_r
            va_out[b] = va_ref[b] * scale + coupling * new_a
        send_out(1, pl.ds(start, part))
        send_out(2, pl.ds(start, part))
    for copy in copies:
        copy.wait()


def struct(shape, dtype=F32):
    return jax.ShapeDtypeStruct(shape, dtype)


def call(kernel, outs, *args, scratch=(), remote=(), loose=(), spec=VMEM):
    specs = [ANY if n in remote else VMEM for n in range(len(args))]
    placed = [x if n in remote or n in loose else pltpu.with_memory_space_constraint(x, pltpu.VMEM) for n, x in enumerate(args)]
    return pl.pallas_call(
        kernel,
        out_shape=outs,
        in_specs=specs,
        out_specs=jax.tree.map(lambda _: spec, outs, is_leaf=lambda x: hasattr(x, "dtype")),
        scratch_shapes=scratch,
    )(*placed)


def xor_pairs(axis, bit):
    return [(i, i ^ bit) for i in range(lax.axis_size(axis))]


def even_pairs(axis):
    return xor_pairs(axis, 1)


def odd_pairs(axis):
    count = lax.axis_size(axis)
    pairs = [(0, count - 1), (count - 1, 0)]
    for i in range(1, count - 1, 2):
        pairs += [(i, i + 1), (i + 1, i)]
    return pairs


def body(rho, vr, va, gas, gvr, gva, stop_time, coef):
    bins, rows, cells = rho.shape
    total = coef.shape[1]
    inner, outer = inner_rows(rows), outer_rows(rows)
    weights_size = (total * bins, 2 * total)
    small = 2 * weights_size[0] * weights_size[1] <= SMALL_BYTES
    weights, gases = call(
        weights_kernel, ((pltpu.VMEM if small else struct)(weights_size, BF16), pltpu.VMEM((3, rows, cells), F32)),
        jnp.transpose(coef, (1, 0, 2)).reshape(total * bins, total), jnp.transpose(coef, (2, 0, 1)).reshape(total * bins, total),
        gas, gvr, gva,
    )
    field, kept = struct(rho.shape), pltpu.VMEM(rho.shape, F32)
    flat = struct(gas.shape)
    halo = pltpu.VMEM((3, bins, cells), BF16)
    inner_lines, outer_lines = lines_of(bins, inner), lines_of(bins, outer)
    halves_in, halves_out = (pltpu.VMEM((6 * len(picked), cells), F32) for picked in (inner, outer))

    edges = [pltpu.VMEM((2 * width, bins, cells), F32) for width in (HALO + 1, HALO, HALO)]
    to_a, to_b, rho_edge, vr_edge, va_edge, table = call(
        load_kernel, (halo, halo, *edges, pltpu.VMEM((2, bins, cells), F32)), rho, vr, va, stop_time[None],
        scratch=[pltpu.VMEM((1, bins), F32), pltpu.SemaphoreType.DMA, pltpu.SemaphoreType.DMA((6 * HALO + 2,))],
        remote=(0, 1, 2, 3),
    )
    from_b = lax.ppermute(to_b, "tile", odd_pairs("tile"))
    from_a = lax.ppermute(to_a, "tile", even_pairs("tile"))

    groups = lax.axis_size("bin")
    half = groups // 2
    dense = [pltpu.VMEM((len(picked), bins, cells), F32) for picked in (inner, outer)]
    low_in, plain_in, adv_in, part_out = call(
        inner_kernel,
        (pltpu.VMEM((inner_lines, cells), BF16), pltpu.VMEM((bins * len(inner), cells), BF16), *dense), table, rho, vr, va,
        scratch=[kept, halves_in],
    )
    near_in = [lax.ppermute(plain_in, "bin", xor_pairs("bin", at)) for at in range(1, half)]
    far_in = lax.ppermute(low_in, "bin", xor_pairs("bin", half))

    adv_out, low_out = call(
        outer_kernel, (dense[1], pltpu.VMEM((outer_lines, cells), BF16)),
        table, rho_edge, vr_edge, va_edge, part_out, from_a, from_b, scratch=[halves_out],
    )
    near_out = [lax.ppermute(low_out, "bin", xor_pairs("bin", at)) for at in range(1, half)]
    far_out = [lax.ppermute(low_out, "bin", xor_pairs("bin", at)) for at in range(half, groups)]
    passing = call(pack_kernel, pltpu.VMEM((inner_lines, cells), BF16), low_in, far_in, scratch=[halves_in] * 2)
    passed_in = [lax.ppermute(passing, "bin", xor_pairs("bin", at)) for at in range(1, half)]

    in_messages = [low_in] + near_in + [far_in] + passed_in
    out_messages = [low_out] + near_out + far_out

    dens = [pltpu.VMEM((len(picked), 2 * total, cells), BF16) for picked in (inner, outer)]
    gains = []
    for n, some in ((0, in_messages[:half + 1]), (1, out_messages[:-1])):
        gains.append(call(
            functools.partial(gain_kernel, groups), dense[n], weights, *some, scratch=dens[n:n + 1], loose=() if small else (0,),
        ))
    gain_out, outer_sums = call(
        last_block_kernel, (dense[1], pltpu.VMEM((3, rows, cells), F32)), weights, gains[1], *out_messages,
        scratch=[dens[1], pltpu.VMEM((groups, 3, rows, cells), F32), halves_out], loose=() if small else (0,),
    )
    pieces = 4
    return call(
        functools.partial(last_kernel, groups, pieces), (field, field, field, flat, flat),
        passing, outer_sums, table, gases, vr, va, weights, adv_in, adv_out, gains[0], gain_out, *in_messages,
        scratch=[kept] * 3 + [pltpu.VMEM(gas.shape, F32)] * 2 + dense[:1] + dens[:1]
        + [pltpu.VMEM((half, 3, rows, cells), F32), halves_in]
        + [pltpu.SemaphoreType.DMA((3 + 2 * pieces,))],
        loose=() if small else (6,), spec=ANY,
    )


def solution(mesh):
    field, flat = P("bin", "tile", None), P("tile", None)
    return jax.shard_map(
        body,
        mesh=mesh,
        in_specs=(field, field, field, flat, flat, flat, P("bin"), P("bin", None, None)),
        out_specs=(field, field, field, flat, flat),
        check_vma=False,
    )
```

```python
import functools

import jax
import jax.numpy as jnp
from jax import lax
from jax.experimental import pallas as pl
from jax.experimental.pallas import tpu as pltpu
from jax.sharding import PartitionSpec as P


COURANT = 0.2
COAGULATION = 0.5
HALO = 2
SMALL_BYTES = 2**19
F32 = jnp.float32
BF16 = jnp.bfloat16

VMEM = pl.BlockSpec(memory_space=pltpu.VMEM)
ANY = pl.BlockSpec(memory_space=pl.ANY)


def minmod(a, b):
    return jnp.maximum(jnp.minimum(a, b), jnp.minimum(jnp.maximum(a, b), 0.0))


def face_flux(low, low_slope, high, high_slope, low_speed, high_speed):
    cu = low_speed + high_speed
    reach = 0.5 - 0.5 * jnp.abs(cu)
    return cu * jnp.where(cu > 0, low + reach * low_slope, high - reach * high_slope)


def shift(x, by, axis):
    return pltpu.roll(x, by % x.shape[axis], axis)


def edge_rows(rows, width):
    return list(range(width)) + list(range(rows - width, rows))


def load_kernel(rho_in, vr_in, va_in, stop_in, to_a_ref, to_b_ref, rho_ref, vr_ref, va_ref, table_ref, stop_ref, stop_sem, sems):
    _, bins, cells = rho_ref.shape
    rows = rho_in.shape[1]
    stop_copy = pltpu.make_async_copy(stop_in, stop_ref, stop_sem)
    copies = []
    for source, target in ((rho_in, rho_ref), (vr_in, vr_ref), (va_in, va_ref)):
        for n, r in enumerate(edge_rows(rows, target.shape[0] // 2)):
            copies.append(pltpu.make_async_copy(source.at[:, r, :], target.at[n], sems.at[len(copies)]))
    for copy in copies:
        copy.start()
    stop_copy.start()
    stop_copy.wait()
    square = (bins, bins)
    own = lax.broadcasted_iota(jnp.int32, square, 0) == lax.broadcasted_iota(jnp.int32, square, 1)
    stop = jnp.sum(jnp.where(own, jnp.broadcast_to(stop_ref[...], square), 0.0), axis=1, keepdims=True)
    rate = 1.0 / stop
    scale = 1.0 / (1.0 + rate)
    table_ref[0] = jnp.broadcast_to(rate * scale, (bins, cells))
    table_ref[1] = jnp.broadcast_to(scale, (bins, cells))
    for copy in copies:
        copy.wait()
    even = lax.axis_index("tile") % 2 == 0
    up = (rho_ref[0], rho_ref[1], vr_ref[0])
    last, last_v = rho_ref.shape[0] - 1, vr_ref.shape[0] - 1
    down = (rho_ref[last], rho_ref[last - 1], vr_ref[last_v])
    for n in range(3):
        to_a_ref[n] = jnp.where(even, down[n], up[n]).astype(BF16)
        to_b_ref[n] = jnp.where(even, up[n], down[n]).astype(BF16)


def radial_inside(q, v):
    rows = q.shape[0]
    row = lax.broadcasted_iota(jnp.int32, q.shape, 0)
    q_next = shift(q, -1, 0)
    d = q_next - q
    s = minmod(shift(d, 1, 0), d)
    flux = face_flux(q, s, q_next, shift(s, -1, 0), v, shift(v, -1, 0))
    flux = jnp.where((row >= HALO - 1) & (row < rows - HALO), flux, 0.0)
    return flux - shift(flux, 1, 0)


def azimuthal(q, v):
    q_next = shift(q, -1, 1)
    d = q_next - q
    s = minmod(shift(d, 1, 1), d)
    flux = face_flux(q, s, q_next, shift(s, -1, 1), v, shift(v, -1, 1))
    return flux - shift(flux, 1, 1)


def inner_rows(rows):
    return list(range(HALO, rows - HALO))


def outer_rows(rows):
    return edge_rows(rows, HALO)


def lines_of(bins, picked):
    return (bins + 6) * len(picked)


def write_message(ref, densities, sums, halves_ref):
    bins, count = densities[0].shape[0], len(densities)
    for m in range(count):
        ref[m * bins:(m + 1) * bins, :] = densities[m].astype(BF16)
        for n in range(3):
            high = sums[n][m].astype(BF16).astype(F32)
            for half, value in enumerate((high, sums[n][m] - high)):
                at = (2 * n + half) * count + m
                halves_ref[at:at + 1, :] = value
    ref[count * bins:, :] = halves_ref[...].astype(BF16)


def read_sums(ref, picked, bins, halves_ref, sums_ref):
    count = len(picked)
    halves_ref[...] = ref[count * bins:, :].astype(F32)
    for n in range(3):
        for m, r in enumerate(picked):
            high, low = 2 * n * count + m, (2 * n + 1) * count + m
            sums_ref[n, r:r + 1, :] = halves_ref[high:high + 1, :] + halves_ref[low:low + 1, :]


def weighed(sums, adv, vr, va, coupling):
    weight = adv * coupling
    return (sums[0] + weight * vr, sums[1] + weight * va, sums[2] + weight)


def inner_kernel(table_ref, rho_ref, vr_ref, va_ref, message_ref, plain_ref, adv_ref, all_ref, halves_ref):
    bins, rows, cells = rho_ref.shape
    zero = jnp.zeros((rows, cells), F32)
    sums = (zero, zero, zero)
    for b in range(bins):
        q, vr, va = rho_ref[b], vr_ref[b], va_ref[b]
        adv = q - (azimuthal(q, 0.5 * COURANT * va) + radial_inside(q, 0.5 * COURANT * vr))
        all_ref[b] = adv
        sums = weighed(sums, adv, vr, va, jnp.broadcast_to(table_ref[0, b:b + 1, :], q.shape))
    picked = inner_rows(rows)
    densities = [all_ref[:, r, :] for r in picked]
    for n, density in enumerate(densities):
        adv_ref[n] = density
    write_message(message_ref, densities, [[x[r:r + 1] for r in picked] for x in sums], halves_ref)
    plain_ref[...] = message_ref[:plain_ref.shape[0], :]


def outer_kernel(table_ref, rho_ref, vr_ref, va_ref, all_ref, from_a_ref, from_b_ref, adv_ref, message_ref, halves_ref):
    tile, tiles = lax.axis_index("tile"), lax.axis_size("tile")
    even = tile % 2 == 0
    has_top = jnp.where(tile > 0, 1.0, 0.0)
    has_bottom = jnp.where(tile < tiles - 1, 1.0, 0.0)
    top, bottom = [], []
    for n in range(3):
        a, b = from_a_ref[n].astype(F32), from_b_ref[n].astype(F32)
        top.append(jnp.where(even, b, a) * has_top)
        bottom.append(jnp.where(even, a, b) * has_bottom)

    def edge(nearest, nearest_part, v, sign, halo):
        q = [halo[1], halo[0]] + nearest
        d = [sign * (q[n] - q[n + 1]) for n in range(4)]
        s = [minmod(d[n], d[n + 1]) for n in range(3)]
        speed = [0.5 * COURANT * x for x in (halo[2], v[0], v[1])]
        flux = []
        for n in range(2):
            low, high = (n, n + 1) if sign < 0 else (n + 1, n)
            flux.append(face_flux(q[low + 1], s[low], q[high + 1], s[high], speed[n], speed[n + 1]))
        outermost = nearest_part[0] - sign * (flux[0] - flux[1])
        return outermost, nearest_part[1] - sign * flux[1]

    row = [rho_ref[n] for n in range(rho_ref.shape[0])]
    speed = [vr_ref[n] for n in range(vr_ref.shape[0])]
    part = [all_ref[:, r, :] for r in outer_rows(all_ref.shape[1])]
    first, second = edge(row[:3], part[:2], speed[:2], -1.0, top)
    last, before = edge(row[:2:-1], part[:1:-1], speed[:1:-1], 1.0, bottom)
    densities = [first, second, before, last]
    sums = [[], [], []]
    for n, density in enumerate(densities):
        adv_ref[n] = density
        weight = density * table_ref[0]
        for kind, value in enumerate((weight * speed[n], weight * va_ref[n], weight)):
            sums[kind].append(jnp.sum(value, axis=0, keepdims=True))
    write_message(message_ref, densities, sums, halves_ref)


def pack_kernel(own_ref, far_ref, out_ref, a_ref, b_ref):
    start = out_ref.shape[0] - a_ref.shape[0]
    count = a_ref.shape[0] // 6
    out_ref[:start, :] = far_ref[:start, :]
    a_ref[...] = own_ref[start:, :].astype(F32)
    b_ref[...] = far_ref[start:, :].astype(F32)
    for n in range(3):
        high, low = pl.ds(2 * n * count, count), pl.ds((2 * n + 1) * count, count)
        both = (a_ref[high, :] + a_ref[low, :]) + (b_ref[high, :] + b_ref[low, :])
        first = both.astype(BF16).astype(F32)
        a_ref[high, :] = first
        a_ref[low, :] = both - first
    out_ref[start:, :] = a_ref[...].astype(BF16)


def total_sums(at, offset, bit):
    if bit == 0:
        return at(offset)
    return total_sums(at, offset, bit // 2) + total_sums(at, offset ^ bit, bit // 2)


def new_gas(passed, total_ref, gases_ref, bins, sums_ref, halves_ref):
    gas = gases_ref[0]
    rows = gas.shape[0]
    for offset, message in enumerate(passed):
        read_sums(message, inner_rows(rows), bins, halves_ref, sums_ref.at[offset])
    row = lax.broadcasted_iota(jnp.int32, gas.shape, 0)
    inside = (row >= HALO) & (row < rows - HALO)
    sums = []
    for n in range(3):
        inner = total_sums(lambda o, n=n: sums_ref[o, n], 0, len(passed) // 2)
        sums.append(jnp.where(inside, inner, total_ref[n]))
    denom = gas + sums[2]
    return (gas * gases_ref[1] + sums[0]) / denom, (gas * gases_ref[2] + sums[1]) / denom


def weights_kernel(rows_ref, swapped_ref, gas_ref, gvr_ref, gva_ref, out_ref, gases_ref):
    for n, ref in enumerate((gas_ref, gvr_ref, gva_ref)):
        gases_ref[n] = ref[...]
    lines, total = rows_ref.shape
    bins = lines // total
    here = lax.axis_index("bin")
    shift_of = (bins - 1).bit_length()
    taker = lax.shift_right_logical(lax.broadcasted_iota(jnp.int32, (lines, total), 0), 2 * shift_of) ^ here
    giver = lax.shift_right_logical(lax.broadcasted_iota(jnp.int32, (lines, total), 1), shift_of) ^ here
    one = rows_ref[...].astype(F32)
    both = one + swapped_ref[...].astype(F32)
    high = both.astype(BF16).astype(F32)
    earlier = giver < taker
    zero = jnp.zeros_like(one)
    out_ref[:, :total] = jnp.where(giver == taker, one, jnp.where(earlier, high, zero)).astype(BF16)
    out_ref[:, total:] = jnp.where(earlier, both - high, zero).astype(BF16)


def block_start(offset, bins):
    return pl.multiple_of((lax.axis_index("bin") ^ offset) * bins, bins)


def add_blocks(weights_ref, messages, count, first, last, dens_ref, gain_ref, old_ref):
    n_rows, bins, cells = gain_ref.shape
    total = dens_ref.shape[1] // 2
    group = 8
    for offset in range(count):
        at = block_start(offset, bins)
        for n in range(n_rows):
            if offset < last:
                low = messages[offset][n * bins:(n + 1) * bins, :]
            else:
                low = jnp.zeros((bins, cells), BF16)
            dens_ref[n, pl.ds(at, bins), :] = low
            dens_ref[n, pl.ds(total + at, bins), :] = low
    for n in range(n_rows):
        both = dens_ref[n]
        acc = jnp.zeros((bins, cells), F32) if old_ref is None else old_ref[n]
        for offset in range(first, last):
            wide = messages[offset][n * bins:(n + 1) * bins, :].astype(F32)
            at = block_start(offset, bins) * bins
            for i in range(0, bins, group):
                lines = pl.ds(pl.multiple_of(at + i * bins, group * bins), group * bins)
                inner = jnp.dot(weights_ref[lines, :], both, preferred_element_type=F32)
                for g in range(group):
                    acc = acc + inner[g * bins:(g + 1) * bins] * wide[i + g:i + g + 1]
        gain_ref[n] = acc


def gain_kernel(count, weights_ref, *refs):
    messages, (gain_ref, dens_ref) = refs[:-2], refs[-2:]
    add_blocks(weights_ref, messages, count, 0, len(messages), dens_ref, gain_ref, None)


def last_block_kernel(weights_ref, old_ref, *refs):
    messages, (gain_ref, total_ref, dens_ref, sums_ref, halves_ref) = refs[:-5], refs[-5:]
    count, bins = len(messages), gain_ref.shape[1]
    add_blocks(weights_ref, messages, count, count - 1, count, dens_ref, gain_ref, old_ref)
    for offset in range(count):
        read_sums(messages[offset], outer_rows(total_ref.shape[1]), bins, halves_ref, sums_ref.at[offset])
    for n in range(3):
        total_ref[n] = total_sums(lambda o, n=n: sums_ref[o, n], 0, count // 2)


def last_kernel(
    count, pieces, passing_ref, total_ref, table_ref, gases_ref, vr_ref, va_ref, weights_ref, adv_in_ref, adv_out_ref,
    gain_in_ref, gain_out_ref, *refs
):
    messages, refs = refs[:count], refs[count:]
    outs, kept, (new_in_ref, dens_ref, sums_ref, halves_ref, sems) = refs[:5], refs[5:10], refs[10:]
    density_ref, vr_out, va_out, gvr_out, gva_out = kept
    bins, rows, _ = vr_ref.shape
    copies = []

    def send_out(n, part=None):
        source, target = (kept[n], outs[n]) if part is None else (kept[n].at[part], outs[n].at[part])
        copies.append(pltpu.make_async_copy(source, target, sems.at[len(copies)]))
        copies[-1].start()

    add_blocks(weights_ref, messages, count, count // 2 + 1, count, dens_ref, new_in_ref, gain_in_ref)
    for n, r in enumerate(inner_rows(rows)):
        density_ref[:, r, :] = adv_in_ref[n] + COAGULATION * new_in_ref[n]
    for n, r in enumerate(outer_rows(rows)):
        density_ref[:, r, :] = adv_out_ref[n] + COAGULATION * gain_out_ref[n]
    send_out(0)
    passed = (passing_ref, *messages[count // 2 + 1:])
    new_r, new_a = new_gas(passed, total_ref, gases_ref, bins, sums_ref, halves_ref)
    gvr_out[...] = new_r
    gva_out[...] = new_a
    send_out(3)
    send_out(4)
    part = bins // pieces
    for start in range(0, bins, part):
        for b in range(start, start + part):
            coupling = jnp.broadcast_to(table_ref[0, b:b + 1, :], new_r.shape)
            scale = jnp.broadcast_to(table_ref[1, b:b + 1, :], new_r.shape)
            vr_out[b] = vr_ref[b] * scale + coupling * new_r
            va_out[b] = va_ref[b] * scale + coupling * new_a
        send_out(1, pl.ds(start, part))
        send_out(2, pl.ds(start, part))
    for copy in copies:
        copy.wait()


def struct(shape, dtype=F32):
    return jax.ShapeDtypeStruct(shape, dtype)


def call(kernel, outs, *args, scratch=(), remote=(), loose=(), spec=VMEM):
    specs = [ANY if n in remote else VMEM for n in range(len(args))]
    placed = [x if n in remote or n in loose else pltpu.with_memory_space_constraint(x, pltpu.VMEM) for n, x in enumerate(args)]
    return pl.pallas_call(
        kernel,
        out_shape=outs,
        in_specs=specs,
        out_specs=jax.tree.map(lambda _: spec, outs, is_leaf=lambda x: hasattr(x, "dtype")),
        scratch_shapes=scratch,
    )(*placed)


def xor_pairs(axis, bit):
    return [(i, i ^ bit) for i in range(lax.axis_size(axis))]


def even_pairs(axis):
    return xor_pairs(axis, 1)


def odd_pairs(axis):
    count = lax.axis_size(axis)
    pairs = [(0, count - 1), (count - 1, 0)]
    for i in range(1, count - 1, 2):
        pairs += [(i, i + 1), (i + 1, i)]
    return pairs


def body(rho, vr, va, gas, gvr, gva, stop_time, coef):
    bins, rows, cells = rho.shape
    total = coef.shape[1]
    inner, outer = inner_rows(rows), outer_rows(rows)
    weights_size = (total * bins, 2 * total)
    small = 2 * weights_size[0] * weights_size[1] <= SMALL_BYTES
    weights, gases = call(
        weights_kernel, ((pltpu.VMEM if small else struct)(weights_size, BF16), pltpu.VMEM((3, rows, cells), F32)),
        jnp.transpose(coef, (1, 0, 2)).reshape(total * bins, total), jnp.transpose(coef, (2, 0, 1)).reshape(total * bins, total),
        gas, gvr, gva,
    )
    field, kept = struct(rho.shape), pltpu.VMEM(rho.shape, F32)
    flat = struct(gas.shape)
    halo = pltpu.VMEM((3, bins, cells), BF16)
    inner_lines, outer_lines = lines_of(bins, inner), lines_of(bins, outer)
    halves_in, halves_out = (pltpu.VMEM((6 * len(picked), cells), F32) for picked in (inner, outer))

    edges = [pltpu.VMEM((2 * width, bins, cells), F32) for width in (HALO + 1, HALO, HALO)]
    to_a, to_b, rho_edge, vr_edge, va_edge, table = call(
        load_kernel, (halo, halo, *edges, pltpu.VMEM((2, bins, cells), F32)), rho, vr, va, stop_time[None],
        scratch=[pltpu.VMEM((1, bins), F32), pltpu.SemaphoreType.DMA, pltpu.SemaphoreType.DMA((6 * HALO + 2,))],
        remote=(0, 1, 2, 3),
    )
    from_b = lax.ppermute(to_b, "tile", odd_pairs("tile"))
    from_a = lax.ppermute(to_a, "tile", even_pairs("tile"))

    groups = lax.axis_size("bin")
    half = groups // 2
    dense = [pltpu.VMEM((len(picked), bins, cells), F32) for picked in (inner, outer)]
    low_in, plain_in, adv_in, part_all = call(
        inner_kernel,
        (pltpu.VMEM((inner_lines, cells), BF16), pltpu.VMEM((bins * len(inner), cells), BF16), dense[0], kept), table, rho, vr, va,
        scratch=[halves_in],
    )
    near_in = [lax.ppermute(plain_in, "bin", xor_pairs("bin", at)) for at in range(1, half)]
    far_in = lax.ppermute(low_in, "bin", xor_pairs("bin", half))

    adv_out, low_out = call(
        outer_kernel, (dense[1], pltpu.VMEM((outer_lines, cells), BF16)),
        table, rho_edge, vr_edge, va_edge, part_all, from_a, from_b, scratch=[halves_out],
    )
    near_out = [lax.ppermute(low_out, "bin", xor_pairs("bin", at)) for at in range(1, half)]
    far_out = [lax.ppermute(low_out, "bin", xor_pairs("bin", at)) for at in range(half, groups)]
    passing = call(pack_kernel, pltpu.VMEM((inner_lines, cells), BF16), low_in, far_in, scratch=[halves_in] * 2)
    passed_in = [lax.ppermute(passing, "bin", xor_pairs("bin", at)) for at in range(1, half)]

    in_messages = [low_in] + near_in + [far_in] + passed_in
    out_messages = [low_out] + near_out + far_out

    dens = [pltpu.VMEM((len(picked), 2 * total, cells), BF16) for picked in (inner, outer)]
    gains = []
    for n, some in ((0, in_messages[:half + 1]), (1, out_messages[:-1])):
        gains.append(call(
            functools.partial(gain_kernel, groups), dense[n], weights, *some, scratch=dens[n:n + 1], loose=() if small else (0,),
        ))
    gain_out, outer_sums = call(
        last_block_kernel, (dense[1], pltpu.VMEM((3, rows, cells), F32)), weights, gains[1], *out_messages,
        scratch=[dens[1], pltpu.VMEM((groups, 3, rows, cells), F32), halves_out], loose=() if small else (0,),
    )
    pieces = 4
    return call(
        functools.partial(last_kernel, groups, pieces), (field, field, field, flat, flat),
        passing, outer_sums, table, gases, vr, va, weights, adv_in, adv_out, gains[0], gain_out, *in_messages,
        scratch=[kept] * 3 + [pltpu.VMEM(gas.shape, F32)] * 2 + dense[:1] + dens[:1]
        + [pltpu.VMEM((half, 3, rows, cells), F32), halves_in]
        + [pltpu.SemaphoreType.DMA((3 + 2 * pieces,))],
        loose=() if small else (6,), spec=ANY,
    )


def solution(mesh):
    field, flat = P("bin", "tile", None), P("tile", None)
    return jax.shard_map(
        body,
        mesh=mesh,
        in_specs=(field, field, field, flat, flat, flat, P("bin"), P("bin", None, None)),
        out_specs=(field, field, field, flat, flat),
        check_vma=False,
    )
```
